128 devices in a mesh: tile: 32 (over y, z, core), row: 4 (over x).
Axes of the slice: x: 4, y: 4, z: 4, core: 2. Of those that a mesh axis runs over, the one named last changes fastest.
Arguments:
- cam_disp: bfloat16 [4, 32, 4, 2, 256, 512], P('row', 'tile')
- footprint: int32 [4, 32, 2, 2], P('row', 'tile'), may hold values from 0 to 15, as said below
- stencil: int32 [4, 32, 2, 2, 2, 256], P('row', 'tile'), may hold values from 0 to 12
- frac: float32 [4, 32, 2, 2, 2, 256], P('row', 'tile'), may hold values from 0 to 1
- coef: float32 [4, 32, 2, 3, 4, 256], P('row', 'tile'), may hold values from -3 to 3
Outputs:
- velocity: bfloat16 [4, 32, 2, 3, 256, 512], P('row', 'tile')
- rfactor: float32 [512, 512], replicated
The draws below stay inside these ranges and needn't reach their ends.
Inputs may be any that keep to these rules, and one draw needn't show every extreme that they name: `footprint`: for each device, the camera tiles named for camera 0 all lie in one row group and are distinct; those for camera 1 lie in other row groups. So a device needs at most 2 distinct camera tiles from any one row group, and exactly 2 from one of them.
All inputs are finite; a program needn't handle non-finite values.
Results may differ from the reference program's by a relative error of at most 0.0015.
The reference program's roundings to bfloat16 on the way count: a program that leaves them out, or rounds other values in their place, can miss the bound.
Values may be sent and summed in bfloat16 or wider, within the bound.
No kernel may reach another device: no remote copies, remote signals or barrier semaphores. Data moves between devices by JAX's collectives and lax.ppermute only.
A program may use at most 512 MiB of HBM per device.

```python
import jax
import jax.numpy as jnp
from jax import lax

S = 512
TILE_SIDE = 16
WT_DEV = 2
PIX = 256
WC = 256
CAM_DEV = 4
N_TILE = 32
N_ROW = 4


def draw_cam_disp(key, part):
    keys = jax.random.split(jax.random.fold_in(key, 11), 4)
    base = jax.random.normal(keys[0], (N_ROW, N_TILE, CAM_DEV, 2, PIX, 1), jnp.float32)
    scales = jnp.exp(jax.random.uniform(keys[1], (N_ROW, N_TILE, CAM_DEV, 1, 1, 1), jnp.float32, jnp.log(0.5), jnp.log(3.0)))
    noise = jax.random.normal(keys[2], (N_ROW, N_TILE, CAM_DEV, 2, PIX, S), jnp.float32)
    column = jnp.exp(jax.random.uniform(keys[3], (S,), jnp.float32, jnp.log(0.3), jnp.log(3.0)))
    mix = 0.8
    return (scales * column * (mix * base + noise)).astype(jnp.bfloat16)


def draw_footprint(key, part):
    keys = jax.random.split(jax.random.fold_in(key, 23), 4)
    owners = N_ROW * N_TILE
    first_group = jax.random.randint(keys[0], (owners, 1), 0, N_ROW)
    perm_keys = jax.random.split(keys[1], owners)
    local_first = jax.vmap(lambda k: jax.random.permutation(k, CAM_DEV)[:WT_DEV])(perm_keys)
    other = (first_group + 1 + jax.random.randint(keys[2], (owners, WT_DEV), 0, N_ROW - 1)) % N_ROW
    local_second = jax.random.randint(keys[3], (owners, WT_DEV), 0, CAM_DEV)
    first = first_group * CAM_DEV + local_first
    second = other * CAM_DEV + local_second
    both = jnp.stack([first, second], axis=-1)
    return both.reshape(N_ROW, N_TILE, WT_DEV, 2).astype(jnp.int32)


def with_ends(entries, stream_key, smallest, largest):
    longest = entries.shape.index(max(entries.shape))
    spots = []
    for shift in (0, 1):
        where = [jax.random.randint(jax.random.fold_in(stream_key, axis), (), 0, length) for axis, length in enumerate(entries.shape)]
        where[longest] = (where[longest] + shift) % entries.shape[longest]
        spots.append(tuple(where))
    return entries.at[spots[0]].set(smallest).at[spots[1]].set(largest)


def shard_levels(stream_key, extent, shards, low, high):
    level, own = 1.0, jax.random.fold_in(stream_key, 6)
    for position, blocks in shards:
        draws = jnp.exp(jax.random.uniform(jax.random.fold_in(own, position), (blocks,), jnp.float32, low / len(shards), high / len(shards)))
        level = level * jnp.repeat(draws, extent[position] // blocks).reshape([-1 if axis == position else 1 for axis in range(len(extent))])
    return level


def scatter_about(own_key, extent, spread, bound, cuts=(), kind=jnp.bfloat16):
    result = jax.random.normal(own_key, extent, jnp.float32) * spread
    if len(cuts) > 0:
        result = shard_levels(own_key, extent, cuts, -0.22, 0.18) * result
    return jnp.clip(result, min=-bound, max=bound).astype(kind)


def setup_inputs(seed: int = 0) -> dict:
    streams_of = jax.random.split(jax.random.key(seed), 6)
    return {
        "cam_disp": draw_cam_disp(jax.random.fold_in(streams_of[5], 71), 0),
        "footprint": draw_footprint(jax.random.fold_in(streams_of[5], 71), 0),
        "stencil": with_ends(jax.random.randint(streams_of[2], (N_ROW, N_TILE, WT_DEV, 2, 2, WC), 0, TILE_SIDE - 3), jax.random.fold_in(streams_of[2], 1), 0, (TILE_SIDE - 3) - 1).astype(jnp.int32),
        "frac": jnp.clip(1.0 * jax.random.uniform(streams_of[3], (N_ROW, N_TILE, WT_DEV, 2, 2, WC), jnp.float32) ** shard_levels(streams_of[3], (N_ROW, N_TILE, WT_DEV, 2, 2, WC), ((0, 4), (1, 32)), -0.2, 0.2), 0.0, 1.0),
        "coef": scatter_about(streams_of[4], (N_ROW, N_TILE, WT_DEV, 3, 4, WC), 0.5, 3.0, ((0, 4), (1, 32)), jnp.float32),
    }


def catmull(t):
    k0 = ((-0.5 * t + 1.0) * t - 0.5) * t
    k1 = (1.5 * t - 2.5) * t * t + 1.0
    k2 = ((-1.5 * t + 2.0) * t + 0.5) * t
    k3 = (0.5 * t - 0.5) * t * t
    return (k0, k1, k2, k3)

def axis_weights(base, fraction, side):
    positions = jnp.arange(side, dtype=jnp.int32)
    weights = catmull(fraction)
    total = jnp.zeros((base.shape[0], side), jnp.float32)
    for shift in range(4):
        total = total + weights[shift][:, None] * (positions[None, :] == base[:, None] + shift).astype(jnp.float32)
    return total

def interp_matrix(base_pair, frac_pair, side):
    rows = axis_weights(base_pair[0], frac_pair[0], side)
    cols = axis_weights(base_pair[1], frac_pair[1], side)
    whole = rows[:, :, None] * cols[:, None, :]
    return whole.reshape(whole.shape[0], side * side).astype(jnp.bfloat16)

def velocity_tiles(pool, ids, sten, fraction, weights_coef):
    world = weights_coef.shape[0]
    cells = weights_coef.shape[3]
    picked = jnp.take(pool, ids.reshape(-1), axis=0)
    mats = jax.vmap(lambda b, f: interp_matrix(b, f, TILE_SIDE))(sten.reshape(world * 2, 2, cells), fraction.reshape(world * 2, 2, cells))
    interp = jnp.einsum('pqx,pjxs->pjqs', mats.astype(jnp.float32), picked.astype(jnp.float32))
    interp = interp.reshape(world, 4, cells, interp.shape[-1])
    total = jnp.zeros((world, 3, cells, interp.shape[-1]), jnp.float32)
    for inner in range(4):
        total = total + weights_coef[:, :, inner, :, None] * interp[:, None, inner]
    return total.astype(jnp.bfloat16)

def reference(cam_disp, footprint, stencil, frac, coef):
    groups = footprint.shape[0]
    columns = footprint.shape[1]
    snaps = cam_disp.shape[-1]

    def one_device(index):
        grp = (index // columns).astype(jnp.int32)
        col = (index % columns).astype(jnp.int32)
        pool = jnp.take(cam_disp, col, axis=1)
        pool = pool.reshape(groups * cam_disp.shape[2], 2, cam_disp.shape[4], snaps)
        ids = footprint[grp, col]
        vel = velocity_tiles(pool, ids, stencil[grp, col], frac[grp, col], coef[grp, col])
        rows = vel.reshape(-1, snaps)
        gram = jnp.dot(rows.T.astype(jnp.float32), rows.astype(jnp.float32), preferred_element_type=jnp.float32)
        return (vel, gram)
    vels, grams = lax.map(one_device, jnp.arange(groups * columns, dtype=jnp.int32))
    velocity = vels.reshape(footprint.shape[:3] + vels.shape[2:])
    total_rows = groups * columns * vels.shape[1] * 3 * vels.shape[3]
    gram = jnp.sum(grams, axis=0) / jnp.float32(total_rows)
    rfactor = jnp.linalg.cholesky(gram).T
    return (velocity, rfactor)
```

```python
import functools

import jax
import jax.numpy as jnp
from jax import lax
from jax.experimental import pallas as pl
from jax.experimental.pallas import tpu as pltpu
from jax.sharding import Mesh, PartitionSpec as P

F32 = jnp.float32
BF16 = jnp.bfloat16
TILE_SIDE = 16
CHIPS = ("y", "z", "x")
ANY = pl.BlockSpec(memory_space=pl.ANY)
VM = pl.BlockSpec(memory_space=pltpu.VMEM)


def catmull(t):
    k0 = ((-0.5 * t + 1.0) * t - 0.5) * t
    k1 = (1.5 * t - 2.5) * t * t + 1.0
    k2 = ((-1.5 * t + 2.0) * t + 0.5) * t
    k3 = (0.5 * t - 0.5) * t * t
    return (k0, k1, k2, k3)


def axis_weights(base, fraction, side):
    positions = jnp.arange(side, dtype=jnp.int32)
    weights = catmull(fraction)
    total = jnp.zeros(base.shape + (side,), F32)
    for shift in range(4):
        total = total + weights[shift][..., None] * (positions == base[..., None] + shift).astype(F32)
    return total


def world_kernel(w, pick_ref, cam_ref, r1_ref, r2_ref, r3_ref, mats_ref, coef_ref, *rest):
    if w:
        gin_ref, _, vel_ref, gram_ref, tiles, interp, sem = rest
    else:
        vel_ref, gram_ref, tiles, interp, sem = rest
    cells, snaps = vel_ref.shape[2], vel_ref.shape[3]
    for c in range(2):
        dist = pick_ref[2 * (2 * w + c)]
        index = pick_ref[2 * (2 * w + c) + 1]

        @pl.when(dist == 0)
        def _():
            pltpu.make_async_copy(cam_ref.at[index], tiles.at[c], sem.at[c]).start()

        for k, ref in ((1, r1_ref), (2, r2_ref), (3, r3_ref)):

            @pl.when(dist == k)
            def _():
                pltpu.make_async_copy(ref, tiles.at[c], sem.at[c]).start()

    for c in range(2):
        pltpu.make_async_copy(cam_ref.at[0], tiles.at[c], sem.at[c]).wait()
        for j in range(2):
            interp[2 * c + j] = jnp.dot(mats_ref[c], tiles[c, j], preferred_element_type=F32)

    rows = 32

    def cell_rows(step, _):
        q = pl.ds(pl.multiple_of(step * rows, rows), rows)
        parts = [interp[i, q, :] for i in range(4)]
        for k in range(3):
            total = coef_ref[q, 4 * k : 4 * k + 1] * parts[0]
            for i in range(1, 4):
                total = total + coef_ref[q, 4 * k + i : 4 * k + i + 1] * parts[i]
            vel_ref[0, k, q, :] = total.astype(BF16)
        return 0

    lax.fori_loop(0, cells // rows, cell_rows, 0)
    flat = vel_ref[0].reshape(3 * cells, snaps)
    for i in range(snaps // 256):
        left = flat[:, 256 * i : 256 * (i + 1)]
        block = lax.dot_general(left, flat[:, 256 * i :], (((0,), (0,)), ((), ())), preferred_element_type=F32)
        for j in range(2 * i, snaps // 128):
            part = block[:, 128 * j - 256 * i : 128 * (j + 1) - 256 * i]
            where = (j, pl.ds(256 * i, 256))
            if w:
                part = part + gin_ref[where]
            gram_ref[where] = part
        if i:
            for j in range(2 * i):
                gram_ref[j, pl.ds(256 * i, 256)] = jnp.zeros((256, 128), F32)


def world(w, pick, cam, recv, mats, coef, carry):
    snaps, cells = cam.shape[-1], mats.shape[1]
    world_tiles = 2
    in_specs = [pl.BlockSpec(memory_space=pltpu.SMEM)] + [ANY] * 4 + [VM, VM]
    args = [pick, cam, *recv, mats, coef]
    aliases = {}
    if w:
        in_specs += [VM, ANY]
        args += [carry[1], carry[0]]
        aliases = {len(args) - 1: 0}
    return pl.pallas_call(
        functools.partial(world_kernel, w),
        grid=(1,),
        in_specs=in_specs,
        out_specs=(
            pl.BlockSpec((1, 3, cells, snaps), lambda _: (w, 0, 0, 0)),
            pl.BlockSpec((snaps // 128, snaps, 128), lambda _: (0, 0, 0)),
        ),
        out_shape=(
            jax.ShapeDtypeStruct((world_tiles, 3, cells, snaps), BF16),
            jax.ShapeDtypeStruct((snaps // 128, snaps, 128), F32),
        ),
        scratch_shapes=[
            pltpu.VMEM((2, 2, cam.shape[2], snaps), BF16),
            pltpu.VMEM((4, cells, snaps), F32),
            pltpu.SemaphoreType.DMA((2,)),
        ],
        input_output_aliases=aliases,
        compiler_params=pltpu.CompilerParams(vmem_limit_bytes=32 << 20),
        cost_estimate=pl.CostEstimate(flops=700_000_000, bytes_accessed=4_000_000, transcendentals=0),
        name=f"world{w}",
    )(*args)


def inverse_factor(blocks):
    n, width = len(blocks), blocks[0].shape[1]
    lane = lax.broadcasted_iota(jnp.int32, (8, width), 1)
    sub = lax.broadcasted_iota(jnp.int32, (8, width), 0)
    slabs, out = list(blocks), []
    for s in range(n):
        k0 = 8 * s
        a = slabs[s]
        columns = [jnp.broadcast_to(a[:, k0 + j : k0 + j + 1], (8, width)) for j in range(8)]
        c = [[None] * 8 for _ in range(8)]
        for j in range(8):
            for i in range(j + 1):
                c[i][j] = jnp.broadcast_to(columns[j][i : i + 1, :], (8, width))
                c[j][i] = c[i][j]
        inside = (lane >= k0) & (lane < k0 + 8)
        aug = jnp.where(inside, jnp.where(lane - k0 == sub, 1.0, 0.0), a)
        r = [jnp.broadcast_to(aug[i : i + 1, :], (8, width)) for i in range(8)]
        scaled = [None] * 8
        for k in range(8):
            root = lax.rsqrt(c[k][k])
            inverse = root * root
            scaled[k] = r[k] * root
            t = r[k] * inverse
            ct = [None if j <= k else c[k][j] * inverse for j in range(8)]
            new = [row[:] for row in c]
            for i in range(8):
                if i == k:
                    continue
                r[i] = r[i] - c[i][k] * t
                for j in range(k + 1, 8):
                    if k < j < i:
                        continue
                    new[i][j] = c[i][j] - c[i][k] * ct[j]
                    if i > k:
                        new[j][i] = new[i][j]
            for j in range(k + 1, 8):
                new[k][j] = ct[j]
            c = new
            r[k] = t
        slab = scaled[7]
        for k in range(6, -1, -1):
            slab = jnp.where(sub == k, scaled[k], slab)
        out.append(jnp.where(lane < k0 + 8, slab, 0.0))
        for b in range(s + 1, n):
            x = slabs[b]
            total = jnp.where(inside, 0.0, x)
            for k in range(8):
                total = total - jnp.broadcast_to(x[:, k0 + k : k0 + k + 1], (8, width)) * r[k]
            slabs[b] = total
    return out


def exact_dot(a, b, dims):
    return lax.dot_general(a, b, ((dims[:1], dims[1:]), ((), ())), precision=lax.Precision.HIGHEST, preferred_element_type=F32)


def factor_kernel(g_ref, o_ref, s_ref):
    parts, size = g_ref.shape[0], 128
    n = parts * size
    for j in range(parts):
        s_ref[:, j * size : (j + 1) * size] = g_ref[j]
    o_ref[...] = jnp.zeros_like(o_ref)

    def panel(p, _):
        off = pl.multiple_of(p * size, size)
        blocks = [s_ref[pl.ds(off + 8 * i, 8), pl.ds(off, size)] for i in range(size // 8)]
        linv = jnp.concatenate(inverse_factor(blocks), axis=0)
        for q in range(parts):

            @pl.when(p == q)
            def _():
                lo, wide = q * size, n - q * size
                r = exact_dot(linv, s_ref[lo : lo + size, lo:], (1, 0))
                row = lax.broadcasted_iota(jnp.int32, (size, wide), 0)
                col = lax.broadcasted_iota(jnp.int32, (size, wide), 1)
                r = jnp.where(col >= row, r, 0.0)
                o_ref[lo : lo + size, lo:] = r
                if q < parts - 1:
                    t = r[:, size:]
                    s_ref[lo + size :, lo + size :] = s_ref[lo + size :, lo + size :] - exact_dot(t, t, (0, 0))

        return 0

    lax.fori_loop(0, parts, panel, 0)


def factor(gram):
    n = gram.shape[1]
    return pl.pallas_call(
        factor_kernel,
        out_shape=jax.ShapeDtypeStruct((n, n), F32),
        in_specs=[VM],
        out_specs=VM,
        scratch_shapes=[pltpu.VMEM((n, n), F32)],
        name="factor",
    )(gram)


def sum_devices(gram, scale):
    chips = lax.axis_size("y") * lax.axis_size("z") * lax.axis_size("x")
    flat = gram.reshape(2, -1, 128)
    half = flat.shape[1]
    core = lax.axis_index("core")
    swap = [(0, 1), (1, 0)]
    mine = lax.dynamic_index_in_dim(flat, core, 0, keepdims=False)
    other = lax.dynamic_index_in_dim(flat, 1 - core, 0, keepdims=False)
    mine = mine + lax.ppermute(other, "core", swap)
    pieces = lax.all_to_all(mine.reshape(chips, half // chips, 128), CHIPS, 0, 0)
    piece = jnp.sum(pieces, axis=0) * scale
    whole = lax.all_to_all(jnp.broadcast_to(piece, pieces.shape), CHIPS, 0, 0).reshape(half, 128)
    other = lax.ppermute(whole, "core", swap)
    first = core == 0
    both = jnp.stack([jnp.where(first, whole, other), jnp.where(first, other, whole)])
    return both.reshape(gram.shape)


def local(cam_disp, footprint, stencil, frac, coef):
    cam_count, pix, snaps = cam_disp.shape[2], cam_disp.shape[4], cam_disp.shape[5]
    world_tiles = footprint.shape[2]
    cells = coef.shape[-1]
    groups = lax.axis_size("x")
    me = lax.axis_index("x")
    tiles = cam_disp.reshape(cam_count, 2, pix, snaps)
    ids = footprint.reshape(world_tiles, 2)

    swaps = [[(i, i ^ k) for i in range(groups)] for k in range(groups)]
    asked = [None] + [lax.ppermute(ids, "x", swaps[k]) for k in range(1, groups)]
    received = []
    for w in range(world_tiles):
        got = []
        for k in range(1, groups):
            want = asked[k][w]
            index = jnp.where(want[0] // cam_count == me, want[0], want[1]) % cam_count
            got.append(lax.ppermute(lax.dynamic_index_in_dim(tiles, index, 0, keepdims=False), "x", swaps[k]))
        received.append(got)

    sten = stencil.reshape(world_tiles * 2, 2, cells)
    fraction = frac.reshape(world_tiles * 2, 2, cells)
    row_weights = axis_weights(sten[:, 0], fraction[:, 0], TILE_SIDE)
    col_weights = axis_weights(sten[:, 1], fraction[:, 1], TILE_SIDE)
    mats = (row_weights[:, :, :, None] * col_weights[:, :, None, :]).reshape(world_tiles, 2, cells, pix).astype(BF16)
    coef_cells = coef.reshape(world_tiles, 12, cells).transpose(0, 2, 1)
    pick = jnp.stack([(ids // cam_count) ^ me, ids % cam_count], axis=-1).reshape(-1)

    carry = None
    for w in range(world_tiles):
        carry = world(w, pick, tiles, received[w], mats[w], coef_cells[w], carry)
    velocity, gram = carry
    total_rows = groups * lax.axis_size("y") * lax.axis_size("z") * 2 * world_tiles * 3 * cells
    gram = sum_devices(gram, F32(1.0 / total_rows))
    return (velocity.reshape(1, 1, world_tiles, 3, cells, snaps), factor(gram))


def solution(mesh):
    grid = Mesh(mesh.devices.reshape(4, 4, 2, 4), ("y", "z", "core", "x"))
    columns = ("y", "z", "core")
    in_specs = (
        P("x", columns, None, None, None, None),
        P("x", columns, None, None),
        P("x", columns, None, None, None, None),
        P("x", columns, None, None, None, None),
        P("x", columns, None, None, None, None),
    )
    out_specs = (P("x", columns, None, None, None, None), P())
    return jax.shard_map(local, mesh=grid, in_specs=in_specs, out_specs=out_specs, check_vma=False)
```

```python
import functools

import jax
import jax.numpy as jnp
from jax import lax
from jax.experimental import pallas as pl
from jax.experimental.pallas import tpu as pltpu
from jax.sharding import Mesh, PartitionSpec as P

F32 = jnp.float32
BF16 = jnp.bfloat16
TILE_SIDE = 16
CHIPS = ("y", "z", "x")
ANY = pl.BlockSpec(memory_space=pl.ANY)
VM = pl.BlockSpec(memory_space=pltpu.VMEM)


def catmull(t):
    k0 = ((-0.5 * t + 1.0) * t - 0.5) * t
    k1 = (1.5 * t - 2.5) * t * t + 1.0
    k2 = ((-1.5 * t + 2.0) * t + 0.5) * t
    k3 = (0.5 * t - 0.5) * t * t
    return (k0, k1, k2, k3)


def axis_weights(base, fraction, side):
    positions = jnp.arange(side, dtype=jnp.int32)
    weights = catmull(fraction)
    total = jnp.zeros(base.shape + (side,), F32)
    for shift in range(4):
        total = total + weights[shift][..., None] * (positions == base[..., None] + shift).astype(F32)
    return total


def select_kernel(ids_ref, cam_ref, *rest):
    outs, sem = rest[:-1], rest[-1]
    me = lax.axis_index("x")
    count = cam_ref.shape[0]
    for w, out in enumerate(outs):
        first, second = ids_ref[w, 0], ids_ref[w, 1]
        own = lax.shift_right_logical(first, 2) == me
        index = jnp.where(own, first, second) & (count - 1)
        pltpu.make_async_copy(cam_ref.at[index], out, sem.at[w]).start()
    for w, out in enumerate(outs):
        pltpu.make_async_copy(cam_ref.at[0], out, sem.at[w]).wait()


def select(ids, tiles, k):
    world_tiles = ids.shape[0]
    return pl.pallas_call(
        select_kernel,
        out_shape=[jax.ShapeDtypeStruct(tiles.shape[1:], tiles.dtype)] * world_tiles,
        in_specs=[pl.BlockSpec(memory_space=pltpu.SMEM), ANY],
        out_specs=[VM] * world_tiles,
        scratch_shapes=[pltpu.SemaphoreType.DMA((world_tiles,))],
        cost_estimate=pl.CostEstimate(flops=0, bytes_accessed=2_000_000, transcendentals=0),
        name=f"select{k}",
    )(ids, tiles)


def world_kernel(w, ids_ref, cam_ref, r1_ref, r2_ref, r3_ref, mats_ref, coef_ref, *rest):
    if w:
        gin_ref, _, vel_ref, gram_ref, tiles, interp, sem = rest
    else:
        vel_ref, gram_ref, tiles, interp, sem = rest
    cells, snaps = vel_ref.shape[2], vel_ref.shape[3]
    for c in range(2):
        tile = ids_ref[w, c]
        dist = lax.shift_right_logical(tile, 2) ^ lax.axis_index("x")
        index = tile & 3

        @pl.when(dist == 0)
        def _():
            pltpu.make_async_copy(cam_ref.at[index], tiles.at[c], sem.at[c]).start()

        for k, ref in ((1, r1_ref), (2, r2_ref), (3, r3_ref)):

            @pl.when(dist == k)
            def _():
                pltpu.make_async_copy(ref, tiles.at[c], sem.at[c]).start()

    for c in range(2):
        pltpu.make_async_copy(cam_ref.at[0], tiles.at[c], sem.at[c]).wait()
        for j in range(2):
            interp[2 * c + j] = jnp.dot(mats_ref[c], tiles[c, j], preferred_element_type=F32)

    rows = 32

    def cell_rows(step, _):
        q = pl.ds(pl.multiple_of(step * rows, rows), rows)
        parts = [interp[i, q, :] for i in range(4)]
        for k in range(3):
            total = coef_ref[q, 4 * k : 4 * k + 1] * parts[0]
            for i in range(1, 4):
                total = total + coef_ref[q, 4 * k + i : 4 * k + i + 1] * parts[i]
            vel_ref[0, k, q, :] = total.astype(BF16)
        return 0

    lax.fori_loop(0, cells // rows, cell_rows, 0)
    flat = vel_ref[0].reshape(3 * cells, snaps)
    for i in range(snaps // 256):
        left = flat[:, 256 * i : 256 * (i + 1)]
        block = lax.dot_general(left, flat[:, 256 * i :], (((0,), (0,)), ((), ())), preferred_element_type=F32)
        for j in range(2 * i, snaps // 128):
            part = block[:, 128 * j - 256 * i : 128 * (j + 1) - 256 * i]
            where = (j, pl.ds(256 * i, 256))
            if w:
                part = part + gin_ref[where]
            gram_ref[where] = part
        if i:
            for j in range(2 * i):
                gram_ref[j, pl.ds(256 * i, 256)] = jnp.zeros((256, 128), F32)


def world(w, ids, cam, recv, mats, coef, carry):
    snaps, cells = cam.shape[-1], mats.shape[1]
    world_tiles = 2
    in_specs = [pl.BlockSpec(memory_space=pltpu.SMEM)] + [ANY] * 4 + [VM, VM]
    args = [ids, cam, *recv, mats, coef]
    aliases = {}
    if w:
        in_specs += [VM, ANY]
        args += [carry[1], carry[0]]
        aliases = {len(args) - 1: 0}
    return pl.pallas_call(
        functools.partial(world_kernel, w),
        grid=(1,),
        in_specs=in_specs,
        out_specs=(
            pl.BlockSpec((1, 3, cells, snaps), lambda _: (w, 0, 0, 0)),
            pl.BlockSpec((snaps // 128, snaps, 128), lambda _: (0, 0, 0)),
        ),
        out_shape=(
            jax.ShapeDtypeStruct((world_tiles, 3, cells, snaps), BF16),
            jax.ShapeDtypeStruct((snaps // 128, snaps, 128), F32),
        ),
        scratch_shapes=[
            pltpu.VMEM((2, 2, cam.shape[2], snaps), BF16),
            pltpu.VMEM((4, cells, snaps), F32),
            pltpu.SemaphoreType.DMA((2,)),
        ],
        input_output_aliases=aliases,
        compiler_params=pltpu.CompilerParams(vmem_limit_bytes=32 << 20),
        cost_estimate=pl.CostEstimate(flops=700_000_000, bytes_accessed=4_000_000, transcendentals=0),
        name=f"world{w}",
    )(*args)


def inverse_factor(blocks):
    n, width = len(blocks), blocks[0].shape[1]
    lane = lax.broadcasted_iota(jnp.int32, (8, width), 1)
    sub = lax.broadcasted_iota(jnp.int32, (8, width), 0)
    slabs, out = list(blocks), []
    for s in range(n):
        k0 = 8 * s
        a = slabs[s]
        columns = [jnp.broadcast_to(a[:, k0 + j : k0 + j + 1], (8, width)) for j in range(8)]
        c = [[None] * 8 for _ in range(8)]
        for j in range(8):
            for i in range(j + 1):
                c[i][j] = jnp.broadcast_to(columns[j][i : i + 1, :], (8, width))
                c[j][i] = c[i][j]
        inside = (lane >= k0) & (lane < k0 + 8)
        aug = jnp.where(inside, jnp.where(lane - k0 == sub, 1.0, 0.0), a)
        r = [jnp.broadcast_to(aug[i : i + 1, :], (8, width)) for i in range(8)]
        scaled = [None] * 8
        for k in range(8):
            root = lax.rsqrt(c[k][k])
            inverse = root * root
            scaled[k] = r[k] * root
            t = r[k] * inverse
            ct = [None if j <= k else c[k][j] * inverse for j in range(8)]
            new = [row[:] for row in c]
            for i in range(8):
                if i == k:
                    continue
                r[i] = r[i] - c[i][k] * t
                for j in range(k + 1, 8):
                    if k < j < i:
                        continue
                    new[i][j] = c[i][j] - c[i][k] * ct[j]
                    if i > k:
                        new[j][i] = new[i][j]
            for j in range(k + 1, 8):
                new[k][j] = ct[j]
            c = new
            r[k] = t
        slab = scaled[7]
        for k in range(6, -1, -1):
            slab = jnp.where(sub == k, scaled[k], slab)
        out.append(jnp.where(lane < k0 + 8, slab, 0.0))
        for b in range(s + 1, n):
            x = slabs[b]
            total = jnp.where(inside, 0.0, x)
            for k in range(8):
                total = total - jnp.broadcast_to(x[:, k0 + k : k0 + k + 1], (8, width)) * r[k]
            slabs[b] = total
    return out


def exact_dot(a, b, dims):
    return lax.dot_general(a, b, ((dims[:1], dims[1:]), ((), ())), precision=lax.Precision.HIGHEST, preferred_element_type=F32)


def factor_kernel(g_ref, o_ref, s_ref):
    parts, size = g_ref.shape[0], 128
    n = parts * size
    for j in range(parts):
        s_ref[:, j * size : (j + 1) * size] = g_ref[j]
    o_ref[...] = jnp.zeros_like(o_ref)

    def panel(p, _):
        off = pl.multiple_of(p * size, size)
        blocks = [s_ref[pl.ds(off + 8 * i, 8), pl.ds(off, size)] for i in range(size // 8)]
        linv = jnp.concatenate(inverse_factor(blocks), axis=0)
        for q in range(parts):

            @pl.when(p == q)
            def _():
                lo, wide = q * size, n - q * size
                r = exact_dot(linv, s_ref[lo : lo + size, lo:], (1, 0))
                row = lax.broadcasted_iota(jnp.int32, (size, wide), 0)
                col = lax.broadcasted_iota(jnp.int32, (size, wide), 1)
                r = jnp.where(col >= row, r, 0.0)
                o_ref[lo : lo + size, lo:] = r
                if q < parts - 1:
                    t = r[:, size:]
                    s_ref[lo + size :, lo + size :] = s_ref[lo + size :, lo + size :] - exact_dot(t, t, (0, 0))

        return 0

    lax.fori_loop(0, parts, panel, 0)


def factor(gram):
    n = gram.shape[1]
    return pl.pallas_call(
        factor_kernel,
        out_shape=jax.ShapeDtypeStruct((n, n), F32),
        in_specs=[VM],
        out_specs=VM,
        scratch_shapes=[pltpu.VMEM((n, n), F32)],
        name="factor",
    )(gram)


def sum_devices(gram, scale):
    chips = lax.axis_size("y") * lax.axis_size("z") * lax.axis_size("x")
    flat = gram.reshape(2, -1, 128)
    half = flat.shape[1]
    core = lax.axis_index("core")
    swap = [(0, 1), (1, 0)]
    mine = lax.dynamic_index_in_dim(flat, core, 0, keepdims=False)
    other = lax.dynamic_index_in_dim(flat, 1 - core, 0, keepdims=False)
    mine = mine + lax.ppermute(other, "core", swap)
    pieces = lax.all_to_all(mine.reshape(chips, half // chips, 128), CHIPS, 0, 0)
    piece = jnp.sum(pieces, axis=0) * scale
    whole = lax.all_to_all(jnp.broadcast_to(piece, pieces.shape), CHIPS, 0, 0).reshape(half, 128)
    other = lax.ppermute(whole, "core", swap)
    first = core == 0
    both = jnp.stack([jnp.where(first, whole, other), jnp.where(first, other, whole)])
    return both.reshape(gram.shape)


def local(cam_disp, footprint, stencil, frac, coef):
    cam_count, pix, snaps = cam_disp.shape[2], cam_disp.shape[4], cam_disp.shape[5]
    world_tiles = footprint.shape[2]
    cells = coef.shape[-1]
    groups = lax.axis_size("x")
    tiles = cam_disp.reshape(cam_count, 2, pix, snaps)
    ids = footprint.reshape(world_tiles, 2)

    swaps = [[(i, i ^ k) for i in range(groups)] for k in range(groups)]
    asked = [None] + [lax.ppermute(ids, "x", swaps[k]) for k in range(1, groups)]
    received = [[None] * groups for _ in range(world_tiles)]
    for k in (2, 1, 3):
        for w, sent in enumerate(select(asked[k], tiles, k)):
            received[w][k] = lax.ppermute(sent, "x", swaps[k])

    sten = stencil.reshape(world_tiles * 2, 2, cells)
    fraction = frac.reshape(world_tiles * 2, 2, cells)
    row_weights = axis_weights(sten[:, 0], fraction[:, 0], TILE_SIDE)
    col_weights = axis_weights(sten[:, 1], fraction[:, 1], TILE_SIDE)
    mats = (row_weights[:, :, :, None] * col_weights[:, :, None, :]).reshape(world_tiles, 2, cells, pix).astype(BF16)
    coef_cells = coef.reshape(world_tiles, 12, cells).transpose(0, 2, 1)

    carry = None
    for w in range(world_tiles):
        carry = world(w, ids, tiles, received[w][1:], mats[w], coef_cells[w], carry)
    velocity, gram = carry
    total_rows = groups * lax.axis_size("y") * lax.axis_size("z") * 2 * world_tiles * 3 * cells
    gram = sum_devices(gram, F32(1.0 / total_rows))
    return (velocity.reshape(1, 1, world_tiles, 3, cells, snaps), factor(gram))


def solution(mesh):
    grid = Mesh(mesh.devices.reshape(4, 4, 2, 4), ("y", "z", "core", "x"))
    columns = ("y", "z", "core")
    in_specs = (
        P("x", columns, None, None, None, None),
        P("x", columns, None, None),
        P("x", columns, None, None, None, None),
        P("x", columns, None, None, None, None),
        P("x", columns, None, None, None, None),
    )
    out_specs = (P("x", columns, None, None, None, None), P())
    return jax.shard_map(local, mesh=grid, in_specs=in_specs, out_specs=out_specs, check_vma=False)
```

```python
import functools

import jax
import jax.numpy as jnp
from jax import lax
from jax.experimental import pallas as pl
from jax.experimental.pallas import tpu as pltpu
from jax.sharding import Mesh, PartitionSpec as P

F32 = jnp.float32
BF16 = jnp.bfloat16
TILE_SIDE = 16
CHIPS = ("y", "z", "x")
ANY = pl.BlockSpec(memory_space=pl.ANY)
VM = pl.BlockSpec(memory_space=pltpu.VMEM)


def catmull(t):
    k0 = ((-0.5 * t + 1.0) * t - 0.5) * t
    k1 = (1.5 * t - 2.5) * t * t + 1.0
    k2 = ((-1.5 * t + 2.0) * t + 0.5) * t
    k3 = (0.5 * t - 0.5) * t * t
    return (k0, k1, k2, k3)


def prepare_kernel(sten_ref, frac_ref, coef_ref, mats_ref, columns_ref):
    pairs, cells = sten_ref.shape[0], sten_ref.shape[2]
    pix = mats_ref.shape[3]
    rows = []
    for p in range(pairs):
        for axis in range(2):
            rows.append(sten_ref[p, axis : axis + 1, :].astype(F32))
            rows.extend(catmull(frac_ref[p, axis : axis + 1, :]))
    for w in range(coef_ref.shape[0]):
        rows.append(coef_ref[w])
    used = sum(r.shape[0] for r in rows)
    rows.append(jnp.zeros((128 - used, cells), F32))
    table = jnp.concatenate(rows, axis=0).T
    columns_ref[...] = table
    lane = lax.broadcasted_iota(jnp.int32, (cells, pix), 1)
    spots = ((lane // TILE_SIDE).astype(F32), (lane % TILE_SIDE).astype(F32))
    for p in range(pairs):
        product = None
        for axis in range(2):
            at = 10 * p + 5 * axis
            offset = spots[axis] - table[:, at : at + 1]
            weight = jnp.zeros((cells, pix), F32)
            for shift in range(4):
                weight = jnp.where(offset == float(shift), table[:, at + 1 + shift : at + 2 + shift], weight)
            product = weight if product is None else product * weight
        mats_ref[p // 2, p % 2] = product.astype(BF16)


def prepare(sten, frac, coef, pix):
    pairs, _, cells = sten.shape
    return pl.pallas_call(
        prepare_kernel,
        out_shape=(
            jax.ShapeDtypeStruct((pairs // 2, 2, cells, pix), BF16),
            jax.ShapeDtypeStruct((cells, 128), F32),
        ),
        in_specs=[VM] * 3,
        out_specs=(VM, VM),
        compiler_params=pltpu.CompilerParams(vmem_limit_bytes=8 << 20),
        cost_estimate=pl.CostEstimate(flops=4_000_000, bytes_accessed=1_000_000, transcendentals=0),
        name="prepare",
    )(sten, frac, coef)


def select_kernel(ids_ref, cam_ref, *rest):
    outs, sem = rest[:-1], rest[-1]
    me = lax.axis_index("x")
    count = cam_ref.shape[0]
    for w, out in enumerate(outs):
        first, second = ids_ref[w, 0], ids_ref[w, 1]
        own = lax.shift_right_logical(first, 2) == me
        index = jnp.where(own, first, second) & (count - 1)
        pltpu.make_async_copy(cam_ref.at[index], out, sem.at[w]).start()
    for w, out in enumerate(outs):
        pltpu.make_async_copy(cam_ref.at[0], out, sem.at[w]).wait()


def select(ids, tiles, k):
    world_tiles = ids.shape[0]
    return pl.pallas_call(
        select_kernel,
        out_shape=[pltpu.VMEM(tiles.shape[1:], tiles.dtype)] * world_tiles,
        in_specs=[pl.BlockSpec(memory_space=pltpu.SMEM), ANY],
        out_specs=[VM] * world_tiles,
        scratch_shapes=[pltpu.SemaphoreType.DMA((world_tiles,))],
        compiler_params=pltpu.CompilerParams(vmem_limit_bytes=4 << 20),
        cost_estimate=pl.CostEstimate(flops=0, bytes_accessed=2_000_000, transcendentals=0),
        name=f"select{k}",
    )(ids, tiles)


def world_kernel(w, ids_ref, cam_ref, r1_ref, r2_ref, r3_ref, mats_ref, coef_ref, *rest):
    if w:
        gin_ref, _, vel_ref, mine_ref, other_ref, tiles, interp, sem = rest
    else:
        vel_ref, gram_ref, tiles, interp, sem = rest
    cells, snaps = vel_ref.shape[2], vel_ref.shape[3]
    for c in range(2):
        tile = ids_ref[w, c]
        dist = lax.shift_right_logical(tile, 2) ^ lax.axis_index("x")
        index = tile & 3

        @pl.when(dist == 0)
        def _():
            pltpu.make_async_copy(cam_ref.at[index], tiles.at[c], sem.at[c]).start()

        for k, ref in ((1, r1_ref), (2, r2_ref), (3, r3_ref)):

            @pl.when(dist == k)
            def _():
                pltpu.make_async_copy(ref, tiles.at[c], sem.at[c]).start()

    for c in range(2):
        pltpu.make_async_copy(cam_ref.at[0], tiles.at[c], sem.at[c]).wait()
        for j in range(2):
            interp[2 * c + j] = jnp.dot(mats_ref[w, c], tiles[c, j], preferred_element_type=F32)

    rows = 32

    def cell_rows(step, _):
        q = pl.ds(pl.multiple_of(step * rows, rows), rows)
        parts = [interp[i, q, :] for i in range(4)]
        for k in range(3):
            at = 40 + 12 * w + 4 * k
            total = coef_ref[q, at : at + 1] * parts[0]
            for i in range(1, 4):
                total = total + coef_ref[q, at + i : at + i + 1] * parts[i]
            vel_ref[0, k, q, :] = total.astype(BF16)
        return 0

    lax.fori_loop(0, cells // rows, cell_rows, 0)
    flat = vel_ref[0].reshape(3 * cells, snaps)
    core = lax.axis_index("core")
    for i in range(snaps // 256):
        left = flat[:, 256 * i : 256 * (i + 1)]
        block = lax.dot_general(left, flat[:, 256 * i :], (((0,), (0,)), ((), ())), preferred_element_type=F32)
        for j in range(2 * i, snaps // 128):
            part = block[:, 128 * j - 256 * i : 128 * (j + 1) - 256 * i]
            rows_of = pl.ds(256 * i, 256)
            if w == 0:
                gram_ref[j, rows_of] = part
                continue
            part = part + gin_ref[j, rows_of]
            for ref, side in ((mine_ref, core), (other_ref, 1 - core)):

                @pl.when(side == j // 2)
                def _():
                    ref[j % 2, rows_of] = part

        if i:
            for j in range(2 * i):
                for ref, side in ((gram_ref, None),) if w == 0 else ((mine_ref, core), (other_ref, 1 - core)):
                    zero = jnp.zeros((256, 128), F32)
                    if side is None:
                        ref[j, pl.ds(256 * i, 256)] = zero
                        continue

                    @pl.when(side == j // 2)
                    def _():
                        ref[j % 2, pl.ds(256 * i, 256)] = zero


def world(w, ids, cam, recv, mats, coef, carry):
    snaps, cells = cam.shape[-1], mats.shape[2]
    world_tiles = 2
    outs = 2 if w else 1
    blocks = snaps // 128 // outs
    in_specs = [pl.BlockSpec(memory_space=pltpu.SMEM)] + [ANY] * 4 + [VM, VM]
    args = [ids, cam, *recv, mats, coef]
    aliases = {}
    if w:
        in_specs += [VM, ANY]
        args += [carry[1], carry[0]]
        aliases = {len(args) - 1: 0}
    return pl.pallas_call(
        functools.partial(world_kernel, w),
        grid=(1,),
        in_specs=in_specs,
        out_specs=(
            pl.BlockSpec((1, 3, cells, snaps), lambda _: (w, 0, 0, 0)),
            *[pl.BlockSpec((blocks, snaps, 128), lambda _: (0, 0, 0))] * outs,
        ),
        out_shape=(
            jax.ShapeDtypeStruct((world_tiles, 3, cells, snaps), BF16),
            *[jax.ShapeDtypeStruct((blocks, snaps, 128), F32)] * outs,
        ),
        scratch_shapes=[
            pltpu.VMEM((2, 2, cam.shape[2], snaps), BF16),
            pltpu.VMEM((4, cells, snaps), F32),
            pltpu.SemaphoreType.DMA((2,)),
        ],
        input_output_aliases=aliases,
        compiler_params=pltpu.CompilerParams(vmem_limit_bytes=16 << 20),
        cost_estimate=pl.CostEstimate(flops=700_000_000, bytes_accessed=4_000_000, transcendentals=0),
        name=f"world{w}",
    )(*args)


def inverse_factor(blocks):
    n, width = len(blocks), blocks[0].shape[1]
    lane = lax.broadcasted_iota(jnp.int32, (8, width), 1)
    sub = lax.broadcasted_iota(jnp.int32, (8, width), 0)
    slabs, out = list(blocks), []
    for s in range(n):
        k0 = 8 * s
        a = slabs[s]
        columns = [jnp.broadcast_to(a[:, k0 + j : k0 + j + 1], (8, width)) for j in range(8)]
        c = [[None] * 8 for _ in range(8)]
        for j in range(8):
            for i in range(j + 1):
                c[i][j] = jnp.broadcast_to(columns[j][i : i + 1, :], (8, width))
                c[j][i] = c[i][j]
        inside = (lane >= k0) & (lane < k0 + 8)
        aug = jnp.where(inside, jnp.where(lane - k0 == sub, 1.0, 0.0), a)
        r = [jnp.broadcast_to(aug[i : i + 1, :], (8, width)) for i in range(8)]
        scaled = [None] * 8
        for k in range(8):
            root = lax.rsqrt(c[k][k])
            inverse = root * root
            scaled[k] = r[k] * root
            t = r[k] * inverse
            ct = [None if j <= k else c[k][j] * inverse for j in range(8)]
            new = [row[:] for row in c]
            for i in range(8):
                if i == k:
                    continue
                r[i] = r[i] - c[i][k] * t
                for j in range(k + 1, 8):
                    if k < j < i:
                        continue
                    new[i][j] = c[i][j] - c[i][k] * ct[j]
                    if i > k:
                        new[j][i] = new[i][j]
            for j in range(k + 1, 8):
                new[k][j] = ct[j]
            c = new
            r[k] = t
        slab = scaled[7]
        for k in range(6, -1, -1):
            slab = jnp.where(sub == k, scaled[k], slab)
        out.append(jnp.where(lane < k0 + 8, slab, 0.0))
        for b in range(s + 1, n):
            x = slabs[b]
            total = jnp.where(inside, 0.0, x)
            for k in range(8):
                total = total - jnp.broadcast_to(x[:, k0 + k : k0 + k + 1], (8, width)) * r[k]
            slabs[b] = total
    return out


def exact_dot(a, b, dims):
    return lax.dot_general(a, b, ((dims[:1], dims[1:]), ((), ())), precision=lax.Precision.HIGHEST, preferred_element_type=F32)


def factor_kernel(own_ref, other_ref, o_ref, s_ref):
    half, size = own_ref.shape[0], 128
    parts = 2 * half
    n = parts * size
    core = lax.axis_index("core")
    for first, second, side in ((own_ref, other_ref, 0), (other_ref, own_ref, 1)):

        @pl.when(core == side)
        def _():
            for j in range(parts):
                ref = first if j < half else second
                s_ref[: (j + 1) * size, j * size : (j + 1) * size] = ref[j % half, : (j + 1) * size]

    o_ref[...] = jnp.zeros_like(o_ref)

    def panel(p, _):
        off = pl.multiple_of(p * size, size)
        blocks = [s_ref[pl.ds(off + 8 * i, 8), pl.ds(off, size)] for i in range(size // 8)]
        linv = jnp.concatenate(inverse_factor(blocks), axis=0)
        for q in range(parts):

            @pl.when(p == q)
            def _():
                lo, wide = q * size, n - q * size
                r = exact_dot(linv, s_ref[lo : lo + size, lo:], (1, 0))
                row = lax.broadcasted_iota(jnp.int32, (size, wide), 0)
                col = lax.broadcasted_iota(jnp.int32, (size, wide), 1)
                r = jnp.where(col >= row, r, 0.0)
                o_ref[lo : lo + size, lo:] = r
                if q < parts - 1:
                    for m in range(q + 1, parts):
                        at = m * size
                        t = r[:, at - lo :]
                        s_ref[at : at + size, at:] = s_ref[at : at + size, at:] - exact_dot(t[:, :size], t, (0, 0))

        return 0

    lax.fori_loop(0, parts, panel, 0)


def factor(own, other):
    n = own.shape[1]
    return pl.pallas_call(
        factor_kernel,
        out_shape=jax.ShapeDtypeStruct((n, n), F32),
        in_specs=[VM, VM],
        out_specs=VM,
        scratch_shapes=[pltpu.VMEM((n, n), F32)],
        compiler_params=pltpu.CompilerParams(vmem_limit_bytes=16 << 20),
        name="factor",
    )(own, other)


def sum_devices(mine, other, scale):
    chips = lax.axis_size("y") * lax.axis_size("z") * lax.axis_size("x")
    shape = mine.shape
    swap = [(0, 1), (1, 0)]
    mine = mine + lax.ppermute(other, "core", swap)
    pieces = lax.all_to_all(mine.reshape(chips, -1, 128), CHIPS, 0, 0)
    piece = jnp.sum(pieces, axis=0) * scale
    whole = lax.all_to_all(jnp.broadcast_to(piece, pieces.shape), CHIPS, 0, 0).reshape(shape)
    return whole, lax.ppermute(whole, "core", swap)


def local(cam_disp, footprint, stencil, frac, coef):
    cam_count, pix, snaps = cam_disp.shape[2], cam_disp.shape[4], cam_disp.shape[5]
    world_tiles = footprint.shape[2]
    cells = coef.shape[-1]
    groups = lax.axis_size("x")
    tiles = cam_disp.reshape(cam_count, 2, pix, snaps)
    tiles = pltpu.with_memory_space_constraint(tiles, pltpu.HBM)
    ids = footprint.reshape(world_tiles, 2)

    swaps = [[(i, i ^ k) for i in range(groups)] for k in range(groups)]
    asked = [None] + [lax.ppermute(ids, "x", swaps[k]) for k in range(1, groups)]
    received = [[None] * groups for _ in range(world_tiles)]
    for k in (2, 1, 3):
        for w, sent in enumerate(select(asked[k], tiles, k)):
            received[w][k] = lax.ppermute(sent, "x", swaps[k])

    mats, columns = prepare(
        stencil.reshape(world_tiles * 2, 2, cells),
        frac.reshape(world_tiles * 2, 2, cells),
        coef.reshape(world_tiles, 12, cells),
        pix,
    )

    carry = None
    for w in range(world_tiles):
        carry = world(w, ids, tiles, received[w][1:], mats, columns, carry)
    velocity, mine, other = carry
    total_rows = groups * lax.axis_size("y") * lax.axis_size("z") * 2 * world_tiles * 3 * cells
    halves = sum_devices(mine, other, F32(1.0 / total_rows))
    return (velocity.reshape(1, 1, world_tiles, 3, cells, snaps), factor(*halves))


def solution(mesh):
    grid = Mesh(mesh.devices.reshape(4, 4, 2, 4), ("y", "z", "core", "x"))
    columns = ("y", "z", "core")
    in_specs = (
        P("x", columns, None, None, None, None),
        P("x", columns, None, None),
        P("x", columns, None, None, None, None),
        P("x", columns, None, None, None, None),
        P("x", columns, None, None, None, None),
    )
    out_specs = (P("x", columns, None, None, None, None), P())
    return jax.shard_map(local, mesh=grid, in_specs=in_specs, out_specs=out_specs, check_vma=False)
```

```python
import functools

import jax
import jax.numpy as jnp
from jax import lax
from jax.experimental import pallas as pl
from jax.experimental.pallas import tpu as pltpu
from jax.sharding import Mesh, PartitionSpec as P

F32 = jnp.float32
BF16 = jnp.bfloat16
TILE_SIDE = 16
CUTS = 8
HALVES = (((0, 3), (1, 3), (2, 3), (3, 3), (0, 0)), ((0, 2), (1, 2), (2, 2), (0, 1), (1, 1)))
PLACE = {block: (half, at) for half, blocks in enumerate(HALVES) for at, block in enumerate(blocks)}
PLANE = ("y", "z")
ANY = pl.BlockSpec(memory_space=pl.ANY)
VM = pl.BlockSpec(memory_space=pltpu.VMEM)


def catmull(t):
    k0 = ((-0.5 * t + 1.0) * t - 0.5) * t
    k1 = (1.5 * t - 2.5) * t * t + 1.0
    k2 = ((-1.5 * t + 2.0) * t + 0.5) * t
    k3 = (0.5 * t - 0.5) * t * t
    return (k0, k1, k2, k3)


def prepare_kernel(sten_ref, frac_ref, coef_ref, mats_ref, columns_ref):
    pairs, cells = sten_ref.shape[0], sten_ref.shape[2]
    pix = mats_ref.shape[3]
    rows = []
    for p in range(pairs):
        for axis in range(2):
            rows.append(sten_ref[p, axis : axis + 1, :].astype(F32))
            rows.extend(catmull(frac_ref[p, axis : axis + 1, :]))
    for w in range(coef_ref.shape[0]):
        rows.append(coef_ref[w])
    used = sum(r.shape[0] for r in rows)
    rows.append(jnp.zeros((128 - used, cells), F32))
    table = jnp.concatenate(rows, axis=0).T
    columns_ref[...] = table
    lane = lax.broadcasted_iota(jnp.int32, (cells, pix), 1)
    spots = ((lane // TILE_SIDE).astype(F32), (lane % TILE_SIDE).astype(F32))
    for p in range(pairs):
        product = None
        for axis in range(2):
            at = 10 * p + 5 * axis
            offset = spots[axis] - table[:, at : at + 1]
            weight = jnp.zeros((cells, pix), F32)
            for shift in range(4):
                weight = jnp.where(offset == float(shift), table[:, at + 1 + shift : at + 2 + shift], weight)
            product = weight if product is None else product * weight
        mats_ref[p // 2, p % 2] = product.astype(BF16)


def prepare(sten, frac, coef, pix):
    pairs, _, cells = sten.shape
    return pl.pallas_call(
        prepare_kernel,
        out_shape=(
            jax.ShapeDtypeStruct((pairs // 2, 2, cells, pix), BF16),
            jax.ShapeDtypeStruct((cells, 128), F32),
        ),
        in_specs=[VM] * 3,
        out_specs=(VM, VM),
        compiler_params=pltpu.CompilerParams(vmem_limit_bytes=8 << 20),
        cost_estimate=pl.CostEstimate(flops=4_000_000, bytes_accessed=1_000_000, transcendentals=0),
        name="prepare",
    )(sten, frac, coef)


def select_kernel(ids_ref, cam_ref, *rest):
    outs, sem = rest[:-1], rest[-1]
    me = lax.axis_index("x")
    count, _, pix, _ = cam_ref.shape
    copies = []
    for w, out in enumerate(outs):
        first, second = ids_ref[w, 0], ids_ref[w, 1]
        own = lax.shift_right_logical(first, 2) == me
        index = jnp.where(own, first, second) & (count - 1)
        for piece in range(CUTS):
            j, part = divmod(piece, CUTS // 2)
            rows = pl.ds(part * (2 * pix // CUTS), 2 * pix // CUTS)
            copies.append(pltpu.make_async_copy(cam_ref.at[index, j, rows], out.at[j, rows], sem.at[w, piece]))
            copies[-1].start()
    for copy in copies:
        copy.wait()


def select(ids, tiles, k):
    world_tiles = ids.shape[0]
    return pl.pallas_call(
        select_kernel,
        out_shape=[pltpu.VMEM(tiles.shape[1:], tiles.dtype)] * world_tiles,
        in_specs=[pl.BlockSpec(memory_space=pltpu.SMEM), ANY],
        out_specs=[VM] * world_tiles,
        scratch_shapes=[pltpu.SemaphoreType.DMA((world_tiles, CUTS))],
        compiler_params=pltpu.CompilerParams(vmem_limit_bytes=4 << 20),
        cost_estimate=pl.CostEstimate(flops=0, bytes_accessed=2_000_000, transcendentals=0),
        name=f"select{k}",
    )(ids, tiles)


def world_kernel(w, ids_ref, cam_ref, r1_ref, r2_ref, r3_ref, mats_ref, coef_ref, *rest):
    if w:
        gin_ref, _, vel_ref, mine_ref, other_ref, tiles, interp, sem = rest
    else:
        vel_ref, gram_ref, tiles, interp, sem = rest
    cells, snaps = vel_ref.shape[2], vel_ref.shape[3]
    refs = (None, r1_ref, r2_ref, r3_ref)
    chosen = []
    for c in range(2):
        tile = ids_ref[w, c]
        dist = lax.shift_right_logical(tile, 2) ^ lax.axis_index("x")
        chosen.append(dist)

        @pl.when(dist == 0)
        def _():
            pltpu.make_async_copy(cam_ref.at[tile & 3], tiles.at[c], sem.at[c]).start()

    def interpolate(c, source):
        for j in range(2):
            interp[2 * c + j] = jnp.dot(mats_ref[w, c], source[j], preferred_element_type=F32)

    for c in range(2):
        for k in range(4):

            @pl.when(chosen[c] == k)
            def _():
                if k == 0:
                    pltpu.make_async_copy(cam_ref.at[0], tiles.at[c], sem.at[c]).wait()
                interpolate(c, refs[k] if k else tiles.at[c])

    rows = 32

    def cell_rows(step, _):
        q = pl.ds(pl.multiple_of(step * rows, rows), rows)
        parts = [interp[i, q, :] for i in range(4)]
        for k in range(3):
            at = 40 + 12 * w + 4 * k
            total = coef_ref[q, at : at + 1] * parts[0]
            for i in range(1, 4):
                total = total + coef_ref[q, at + i : at + i + 1] * parts[i]
            vel_ref[0, k, q, :] = total.astype(BF16)
        return 0

    lax.fori_loop(0, cells // rows, cell_rows, 0)
    flat = vel_ref[0].reshape(3 * cells, snaps)
    core = lax.axis_index("core")
    for i in range(snaps // 256):
        left = flat[:, 256 * i : 256 * (i + 1)]
        block = lax.dot_general(left, flat[:, 256 * i :], (((0,), (0,)), ((), ())), preferred_element_type=F32)
        parts = []
        for row in (2 * i, 2 * i + 1):
            for column in range(row, snaps // 128):
                half, at = PLACE[row, column]
                part = block[128 * row - 256 * i : 128 * (row + 1) - 256 * i, 128 * column - 256 * i : 128 * (column + 1) - 256 * i]
                if w == 0:
                    gram_ref[half, at] = part
                else:
                    parts.append((half, at, part + gin_ref[half, at]))
        if w == 0:
            continue
        for side in range(2):

            @pl.when(core == side)
            def _():
                for half, at, part in parts:
                    (mine_ref if half == side else other_ref)[at] = part


def world(w, ids, cam, recv, mats, coef, carry):
    snaps, cells = cam.shape[-1], mats.shape[2]
    world_tiles = 2
    outs = 2 if w else 1
    grams = (len(HALVES[0]), 128, 128) if w else (2, len(HALVES[0]), 128, 128)
    in_specs = [pl.BlockSpec(memory_space=pltpu.SMEM), ANY] + [VM] * 5
    args = [ids, cam, *recv, mats, coef]
    aliases = {}
    if w:
        in_specs += [VM, ANY]
        args += [carry[1], carry[0]]
        aliases = {len(args) - 1: 0}
    return pl.pallas_call(
        functools.partial(world_kernel, w),
        grid=(1,),
        in_specs=in_specs,
        out_specs=(
            pl.BlockSpec((1, 3, cells, snaps), lambda _: (w, 0, 0, 0)),
            *[pl.BlockSpec(grams, lambda _: (0,) * len(grams))] * outs,
        ),
        out_shape=(
            jax.ShapeDtypeStruct((world_tiles, 3, cells, snaps), BF16),
            *[jax.ShapeDtypeStruct(grams, F32)] * outs,
        ),
        scratch_shapes=[
            pltpu.VMEM((2, 2, cam.shape[2], snaps), BF16),
            pltpu.VMEM((4, cells, snaps), F32),
            pltpu.SemaphoreType.DMA((2,)),
        ],
        input_output_aliases=aliases,
        compiler_params=pltpu.CompilerParams(vmem_limit_bytes=16 << 20),
        cost_estimate=pl.CostEstimate(flops=700_000_000, bytes_accessed=4_000_000, transcendentals=0),
        name=f"world{w}",
    )(*args)


def spread(x, k):
    return jnp.broadcast_to(x[k % 8 : k % 8 + 1, :], x.shape)


def inverse_factor(blocks, size=16):
    width, per = blocks[0].shape[1], size // 8
    lane = lax.broadcasted_iota(jnp.int32, (8, width), 1)
    sub = lax.broadcasted_iota(jnp.int32, (8, width), 0)
    is_row = [sub == k for k in range(8)]
    slabs, out = list(blocks), []
    for s in range(len(blocks) // per):
        k0 = size * s
        own = slabs[s * per : (s + 1) * per]
        columns = [[jnp.broadcast_to(a[:, k0 + j : k0 + j + 1], (8, width)) for a in own] for j in range(size)]
        inside = (lane >= k0) & (lane < k0 + size)
        rows = [jnp.where(inside, jnp.where(lane - k0 - 8 * v == sub, 1.0, 0.0), a) for v, a in enumerate(own)]
        scaled = [None] * per
        for k in range(size):
            at, here = k // 8, is_row[k % 8]
            root = lax.rsqrt(spread(columns[k][at], k))
            inverse = root * root
            row = spread(rows[at], k)
            final = row * root
            scaled[at] = final if scaled[at] is None else jnp.where(here, final, scaled[at])
            t = row * inverse
            for j in range(k + 1, size):
                ct = spread(columns[j][at], k) * inverse
                new = [columns[j][v] - columns[k][v] * ct for v in range(per)]
                new[at] = jnp.where(here, ct, new[at])
                columns[j] = new
            new = [rows[v] - columns[k][v] * t for v in range(per)]
            new[at] = jnp.where(here, t, new[at])
            rows = new
        out.extend(jnp.where(lane < k0 + size, x, 0.0) for x in scaled)
        solved = [spread(rows[k // 8], k) for k in range(size)]
        for b in range((s + 1) * per, len(blocks)):
            x = slabs[b]
            totals = [jnp.where(inside, 0.0, x), 0.0]
            for k in range(size):
                totals[k % 2] = totals[k % 2] - jnp.broadcast_to(x[:, k0 + k : k0 + k + 1], (8, width)) * solved[k]
            slabs[b] = totals[0] + totals[1]
    return out


def exact_dot(a, b, dims):
    return lax.dot_general(a, b, ((dims[:1], dims[1:]), ((), ())), precision=lax.Precision.HIGHEST, preferred_element_type=F32)


def factor_kernel(own_ref, other_ref, o_ref, s_ref):
    n, size = o_ref.shape[0], 128
    parts = n // size
    core = lax.axis_index("core")
    for side in range(2):

        @pl.when(core == side)
        def _():
            for half, ref in ((side, own_ref), (1 - side, other_ref)):
                for at, (row, column) in enumerate(HALVES[half]):
                    s_ref[row * size : (row + 1) * size, column * size : (column + 1) * size] = ref[at]

    o_ref[...] = jnp.zeros_like(o_ref)

    def panel(p, _):
        off = pl.multiple_of(p * size, size)
        blocks = [s_ref[pl.ds(off + 8 * i, 8), pl.ds(off, size)] for i in range(size // 8)]
        linv = jnp.concatenate(inverse_factor(blocks), axis=0)
        for q in range(parts):

            @pl.when(p == q)
            def _():
                lo, wide = q * size, n - q * size
                r = exact_dot(linv, s_ref[lo : lo + size, lo:], (1, 0))
                row = lax.broadcasted_iota(jnp.int32, (size, wide), 0)
                col = lax.broadcasted_iota(jnp.int32, (size, wide), 1)
                r = jnp.where(col >= row, r, 0.0)
                o_ref[lo : lo + size, lo:] = r
                if q < parts - 1:
                    for m in range(q + 1, parts):
                        at = m * size
                        t = r[:, at - lo :]
                        s_ref[at : at + size, at:] = s_ref[at : at + size, at:] - exact_dot(t[:, :size], t, (0, 0))

        return 0

    lax.fori_loop(0, parts, panel, 0)


def factor(own, other, n):
    return pl.pallas_call(
        factor_kernel,
        out_shape=jax.ShapeDtypeStruct((n, n), F32),
        in_specs=[VM, VM],
        out_specs=VM,
        scratch_shapes=[pltpu.VMEM((n, n), F32)],
        compiler_params=pltpu.CompilerParams(vmem_limit_bytes=16 << 20),
        name="factor",
    )(own, other)


def sum_devices(mine, other, scale):
    planes = lax.axis_size("y") * lax.axis_size("z")
    groups = lax.axis_size("x")
    shape = mine.shape
    swap = [(0, 1), (1, 0)]
    mine = mine + lax.ppermute(other, "core", swap)
    pieces = lax.all_to_all(mine.reshape(planes, -1, 128), PLANE, 0, 0)
    piece = jnp.sum(pieces, axis=0)
    for k in (1, 2):
        piece = piece + lax.ppermute(piece, "x", [(i, i ^ k) for i in range(groups)])
    whole = lax.all_to_all(jnp.broadcast_to(piece * scale, pieces.shape), PLANE, 0, 0).reshape(shape)
    return whole, lax.ppermute(whole, "core", swap)


def local(cam_disp, footprint, stencil, frac, coef):
    cam_count, pix, snaps = cam_disp.shape[2], cam_disp.shape[4], cam_disp.shape[5]
    world_tiles = footprint.shape[2]
    cells = coef.shape[-1]
    groups = lax.axis_size("x")
    tiles = cam_disp.reshape(cam_count, 2, pix, snaps)
    tiles = pltpu.with_memory_space_constraint(tiles, pltpu.HBM)
    ids = footprint.reshape(world_tiles, 2)

    swaps = [[(i, i ^ k) for i in range(groups)] for k in range(groups)]
    asked = [None] + [lax.ppermute(ids, "x", swaps[k]) for k in range(1, groups)]
    received = [[None] * groups for _ in range(world_tiles)]
    for k in (2, 1, 3):
        for w, sent in enumerate(select(asked[k], tiles, k)):
            received[w][k] = lax.ppermute(sent, "x", swaps[k])

    mats, columns = prepare(
        stencil.reshape(world_tiles * 2, 2, cells),
        frac.reshape(world_tiles * 2, 2, cells),
        coef.reshape(world_tiles, 12, cells),
        pix,
    )

    carry = None
    for w in range(world_tiles):
        carry = world(w, ids, tiles, received[w][1:], mats, columns, carry)
    velocity, mine, other = carry
    total_rows = groups * lax.axis_size("y") * lax.axis_size("z") * 2 * world_tiles * 3 * cells
    halves = sum_devices(mine, other, F32(1.0 / total_rows))
    return (velocity.reshape(1, 1, world_tiles, 3, cells, snaps), factor(*halves, snaps))


def solution(mesh):
    grid = Mesh(mesh.devices.reshape(4, 4, 2, 4), ("y", "z", "core", "x"))
    columns = ("y", "z", "core")
    in_specs = (
        P("x", columns, None, None, None, None),
        P("x", columns, None, None),
        P("x", columns, None, None, None, None),
        P("x", columns, None, None, None, None),
        P("x", columns, None, None, None, None),
    )
    out_specs = (P("x", columns, None, None, None, None), P())
    return jax.shard_map(local, mesh=grid, in_specs=in_specs, out_specs=out_specs, check_vma=False)
```

```python
import functools

import jax
import jax.numpy as jnp
from jax import lax
from jax.experimental import pallas as pl
from jax.experimental.pallas import tpu as pltpu
from jax.sharding import Mesh, PartitionSpec as P


F32 = jnp.float32
BF16 = jnp.bfloat16
TILE_SIDE = 16
EARLY = 32
HALVES = (((0, 3), (1, 3), (2, 3), (3, 3), (0, 0)), ((0, 2), (1, 2), (2, 2), (0, 1), (1, 1)))
PLACE = {block: (half, at) for half, blocks in enumerate(HALVES) for at, block in enumerate(blocks)}
PLANE = ("y", "z")
ANY = pl.BlockSpec(memory_space=pl.ANY)
VM = pl.BlockSpec(memory_space=pltpu.VMEM)


def catmull(t):
    k0 = ((-0.5 * t + 1.0) * t - 0.5) * t
    k1 = (1.5 * t - 2.5) * t * t + 1.0
    k2 = ((-1.5 * t + 2.0) * t + 0.5) * t
    k3 = (0.5 * t - 0.5) * t * t
    return (k0, k1, k2, k3)


def prepare_kernel(sten_ref, frac_ref, coef_ref, mats_ref, columns_ref):
    pairs, cells = sten_ref.shape[0], sten_ref.shape[2]
    pix = mats_ref.shape[3]
    rows = []
    for p in range(pairs):
        for axis in range(2):
            rows.append(sten_ref[p, axis : axis + 1, :].astype(F32))
            rows.extend(catmull(frac_ref[p, axis : axis + 1, :]))
    for w in range(coef_ref.shape[0]):
        rows.append(coef_ref[w])
    used = sum(r.shape[0] for r in rows)
    rows.append(jnp.zeros((128 - used, cells), F32))
    table = jnp.concatenate(rows, axis=0).T
    columns_ref[...] = table
    lane = lax.broadcasted_iota(jnp.int32, (cells, pix), 1)
    spots = ((lane // TILE_SIDE).astype(F32), (lane % TILE_SIDE).astype(F32))
    for p in range(pairs):
        product = None
        for axis in range(2):
            at = 10 * p + 5 * axis
            offset = spots[axis] - table[:, at : at + 1]
            weight = jnp.zeros((cells, pix), F32)
            for shift in range(4):
                weight = jnp.where(offset == float(shift), table[:, at + 1 + shift : at + 2 + shift], weight)
            product = weight if product is None else product * weight
        mats_ref[p // 2, p % 2] = product.astype(BF16)


def prepare(sten, frac, coef, pix):
    pairs, _, cells = sten.shape
    return pl.pallas_call(
        prepare_kernel,
        out_shape=(
            jax.ShapeDtypeStruct((pairs // 2, 2, cells, pix), BF16),
            jax.ShapeDtypeStruct((cells, 128), F32),
        ),
        in_specs=[VM] * 3,
        out_specs=(VM, VM),
        compiler_params=pltpu.CompilerParams(vmem_limit_bytes=8 << 20),
        cost_estimate=pl.CostEstimate(flops=4_000_000, bytes_accessed=1_000_000, transcendentals=0),
        name="prepare",
    )(sten, frac, coef)


def early_kernel(ids_ref, cam_ref, ids_out, out, sem):
    copies = [pltpu.make_async_copy(cam_ref.at[t, :, pl.ds(0, EARLY)], out.at[t], sem.at[t]) for t in range(cam_ref.shape[0])]
    for copy in copies:
        copy.start()
    ids_out[...] = ids_ref[...]
    for copy in copies:
        copy.wait()


def early(ids, tiles):
    count, parts, _, snaps = tiles.shape
    return pl.pallas_call(
        early_kernel,
        out_shape=[jax.ShapeDtypeStruct(ids.shape, ids.dtype), jax.ShapeDtypeStruct((count, parts, EARLY, snaps), tiles.dtype)],
        in_specs=[VM, ANY],
        out_specs=[VM, VM],
        scratch_shapes=[pltpu.SemaphoreType.DMA((count,))],
        compiler_params=pltpu.CompilerParams(vmem_limit_bytes=4 << 20),
        cost_estimate=pl.CostEstimate(flops=0, bytes_accessed=500_000, transcendentals=0),
        name="early",
    )(ids, tiles)


def select_kernel(ids_ref, cam_ref, *rest):
    outs, sem = rest[:-1], rest[-1]
    me = lax.axis_index("x")
    count, _, pix, _ = cam_ref.shape
    copies = []
    for w, out in enumerate(outs):
        first, second = ids_ref[w, 0], ids_ref[w, 1]
        own = lax.shift_right_logical(first, 2) == me
        index = jnp.where(own, first, second) & (count - 1)
        copies.append(pltpu.make_async_copy(cam_ref.at[index, :, pl.ds(EARLY, pix - EARLY)], out, sem.at[w]))
        copies[-1].start()
    for copy in copies:
        copy.wait()


def select(ids, tiles):
    world_tiles = ids.shape[0]
    _, parts, pix, snaps = tiles.shape
    return pl.pallas_call(
        select_kernel,
        out_shape=[jax.ShapeDtypeStruct((parts, pix - EARLY, snaps), tiles.dtype)] * world_tiles,
        in_specs=[pl.BlockSpec(memory_space=pltpu.SMEM), ANY],
        out_specs=[VM] * world_tiles,
        scratch_shapes=[pltpu.SemaphoreType.DMA((world_tiles,))],
        compiler_params=pltpu.CompilerParams(vmem_limit_bytes=4 << 20),
        cost_estimate=pl.CostEstimate(flops=0, bytes_accessed=2_000_000, transcendentals=0),
    )(ids, tiles)


def world_kernel(w, ids_ref, cam_ref, e1_ref, e2_ref, e3_ref, r1_ref, r2_ref, r3_ref, mats_ref, coef_ref, *rest):
    if w:
        gin_ref, _, vel_ref, mine_ref, other_ref, tiles, interp, sem = rest
    else:
        vel_ref, gram_ref, tiles, interp, sem = rest
    cells, snaps = vel_ref.shape[2], vel_ref.shape[3]
    firsts, others = (None, e1_ref, e2_ref, e3_ref), (None, r1_ref, r2_ref, r3_ref)
    indices, dists = [], []
    for c in range(2):
        tile = ids_ref[w, c]
        index, dist = tile & 3, lax.shift_right_logical(tile, 2) ^ lax.axis_index("x")
        indices.append(index)
        dists.append(dist)

        @pl.when(dist == 0)
        def _():
            pltpu.make_async_copy(cam_ref.at[index], tiles.at[c], sem.at[c]).start()

    for c in range(2):
        for k in range(4):

            @pl.when(dists[c] == k)
            def _():
                if k == 0:
                    pltpu.make_async_copy(cam_ref.at[0], tiles.at[c], sem.at[c]).wait()
                else:
                    tiles[c, :, :EARLY] = firsts[k][indices[c]]
                    tiles[c, :, EARLY:] = others[k][...]

        for j in range(2):
            interp[2 * c + j] = jnp.dot(mats_ref[w, c], tiles[c, j], preferred_element_type=F32)

    rows = 32

    def cell_rows(step, _):
        q = pl.ds(pl.multiple_of(step * rows, rows), rows)
        parts = [interp[i, q, :] for i in range(4)]
        for k in range(3):
            at = 40 + 12 * w + 4 * k
            total = coef_ref[q, at : at + 1] * parts[0]
            for i in range(1, 4):
                total = total + coef_ref[q, at + i : at + i + 1] * parts[i]
            vel_ref[0, k, q, :] = total.astype(BF16)
        return 0

    lax.fori_loop(0, cells // rows, cell_rows, 0)
    flat = vel_ref[0].reshape(3 * cells, snaps)
    core = lax.axis_index("core")
    for i in range(snaps // 256):
        left = flat[:, 256 * i : 256 * (i + 1)]
        block = lax.dot_general(left, flat[:, 256 * i :], (((0,), (0,)), ((), ())), preferred_element_type=F32)
        parts = []
        for row in (2 * i, 2 * i + 1):
            for column in range(row, snaps // 128):
                half, at = PLACE[row, column]
                part = block[128 * row - 256 * i : 128 * (row + 1) - 256 * i, 128 * column - 256 * i : 128 * (column + 1) - 256 * i]
                if w == 0:
                    gram_ref[half, at] = part
                else:
                    parts.append((half, at, part + gin_ref[half, at]))
        if w == 0:
            continue
        for side in range(2):

            @pl.when(core == side)
            def _():
                for half, at, part in parts:
                    (mine_ref if half == side else other_ref)[at] = part


def world(w, ids, cam, firsts, recv, mats, coef, carry):
    snaps, cells = cam.shape[-1], mats.shape[2]
    world_tiles = 2
    outs = 2 if w else 1
    grams = (len(HALVES[0]), 128, 128) if w else (2, len(HALVES[0]), 128, 128)
    in_specs = [pl.BlockSpec(memory_space=pltpu.SMEM), ANY] + [VM] * 8
    args = [ids, cam, *firsts, *recv, mats, coef]
    aliases = {}
    if w:
        in_specs += [VM, ANY]
        args += [carry[1], carry[0]]
        aliases = {len(args) - 1: 0}
    return pl.pallas_call(
        functools.partial(world_kernel, w),
        grid=(1,),
        in_specs=in_specs,
        out_specs=(
            pl.BlockSpec((1, 3, cells, snaps), lambda _: (w, 0, 0, 0)),
            *[pl.BlockSpec(grams, lambda _: (0,) * len(grams))] * outs,
        ),
        out_shape=(
            jax.ShapeDtypeStruct((world_tiles, 3, cells, snaps), BF16),
            *[jax.ShapeDtypeStruct(grams, F32)] * outs,
        ),
        scratch_shapes=[
            pltpu.VMEM((2, 2, cam.shape[2], snaps), BF16),
            pltpu.VMEM((4, cells, snaps), F32),
            pltpu.SemaphoreType.DMA((2,)),
        ],
        input_output_aliases=aliases,
        compiler_params=pltpu.CompilerParams(vmem_limit_bytes=16 << 20),
        cost_estimate=pl.CostEstimate(flops=700_000_000, bytes_accessed=4_000_000, transcendentals=0),
    )(*args)


def spread(x, k):
    return jnp.broadcast_to(x[k % 8 : k % 8 + 1, :], x.shape)


def inverse_factor(blocks, size=16):
    width, per = blocks[0].shape[1], size // 8
    lane = lax.broadcasted_iota(jnp.int32, (8, width), 1)
    sub = lax.broadcasted_iota(jnp.int32, (8, width), 0)
    is_row = [sub == k for k in range(8)]
    slabs, out = list(blocks), []
    for s in range(len(blocks) // per):
        k0 = size * s
        own = slabs[s * per : (s + 1) * per]
        columns = [[jnp.broadcast_to(a[:, k0 + j : k0 + j + 1], (8, width)) for a in own] for j in range(size)]
        inside = (lane >= k0) & (lane < k0 + size)
        rows = [jnp.where(inside, jnp.where(lane - k0 - 8 * v == sub, 1.0, 0.0), a) for v, a in enumerate(own)]
        scaled = [None] * per
        for k in range(size):
            at, here = k // 8, is_row[k % 8]
            root = lax.rsqrt(spread(columns[k][at], k))
            inverse = root * root
            row = spread(rows[at], k)
            final = row * root
            scaled[at] = final if scaled[at] is None else jnp.where(here, final, scaled[at])
            t = row * inverse
            for j in range(k + 1, size):
                ct = spread(columns[j][at], k) * inverse
                new = [columns[j][v] - columns[k][v] * ct for v in range(per)]
                new[at] = jnp.where(here, ct, new[at])
                columns[j] = new
            new = [rows[v] - columns[k][v] * t for v in range(per)]
            new[at] = jnp.where(here, t, new[at])
            rows = new
        out.extend(jnp.where(lane < k0 + size, x, 0.0) for x in scaled)
        solved = [spread(rows[k // 8], k) for k in range(size)]
        for b in range((s + 1) * per, len(blocks)):
            x = slabs[b]
            totals = [jnp.where(inside, 0.0, x), 0.0]
            for k in range(size):
                totals[k % 2] = totals[k % 2] - jnp.broadcast_to(x[:, k0 + k : k0 + k + 1], (8, width)) * solved[k]
            slabs[b] = totals[0] + totals[1]
    return out


def exact_dot(a, b, dims):
    return lax.dot_general(a, b, ((dims[:1], dims[1:]), ((), ())), precision=lax.Precision.HIGHEST, preferred_element_type=F32)


def factor_kernel(own_ref, other_ref, o_ref, s_ref):
    n, size = o_ref.shape[0], 128
    parts = n // size
    core = lax.axis_index("core")
    for side in range(2):

        @pl.when(core == side)
        def _():
            for half, ref in ((side, own_ref), (1 - side, other_ref)):
                for at, (row, column) in enumerate(HALVES[half]):
                    s_ref[row * size : (row + 1) * size, column * size : (column + 1) * size] = ref[at]

    o_ref[...] = jnp.zeros_like(o_ref)

    def panel(p, _):
        off = pl.multiple_of(p * size, size)
        blocks = [s_ref[pl.ds(off + 8 * i, 8), pl.ds(off, size)] for i in range(size // 8)]
        linv = jnp.concatenate(inverse_factor(blocks), axis=0)
        for q in range(parts):

            @pl.when(p == q)
            def _():
                lo, wide = q * size, n - q * size
                r = exact_dot(linv, s_ref[lo : lo + size, lo:], (1, 0))
                row = lax.broadcasted_iota(jnp.int32, (size, wide), 0)
                col = lax.broadcasted_iota(jnp.int32, (size, wide), 1)
                r = jnp.where(col >= row, r, 0.0)
                o_ref[lo : lo + size, lo:] = r
                if q < parts - 1:
                    for m in range(q + 1, parts):
                        at = m * size
                        t = r[:, at - lo :]
                        s_ref[at : at + size, at:] = s_ref[at : at + size, at:] - exact_dot(t[:, :size], t, (0, 0))

        return 0

    lax.fori_loop(0, parts, panel, 0)


def factor(own, other, n):
    return pl.pallas_call(
        factor_kernel,
        out_shape=jax.ShapeDtypeStruct((n, n), F32),
        in_specs=[VM, VM],
        out_specs=VM,
        scratch_shapes=[pltpu.VMEM((n, n), F32)],
        compiler_params=pltpu.CompilerParams(vmem_limit_bytes=16 << 20),
        name="factor",
    )(own, other)


def sum_devices(mine, other, scale):
    planes = lax.axis_size("y") * lax.axis_size("z")
    groups = lax.axis_size("x")
    shape = mine.shape
    swap = [(0, 1), (1, 0)]
    mine = mine + lax.ppermute(other, "core", swap)
    pieces = lax.all_to_all(mine.reshape(planes, -1, 128), PLANE, 0, 0)
    piece = jnp.sum(pieces, axis=0)
    for k in (1, 2):
        piece = piece + lax.ppermute(piece, "x", [(i, i ^ k) for i in range(groups)])
    whole = lax.all_to_all(jnp.broadcast_to(piece * scale, pieces.shape), PLANE, 0, 0).reshape(shape)
    return whole, lax.ppermute(whole, "core", swap)


def program(cam_disp, footprint, stencil, frac, coef):
    cam_count, pix, snaps = cam_disp.shape[2], cam_disp.shape[4], cam_disp.shape[5]
    world_tiles = footprint.shape[2]
    cells = coef.shape[-1]
    groups = lax.axis_size("x")
    tiles = cam_disp.reshape(cam_count, 2, pix, snaps)
    tiles = pltpu.with_memory_space_constraint(tiles, pltpu.HBM)
    ids = footprint.reshape(world_tiles, 2)

    swaps = [[(i, i ^ k) for i in range(groups)] for k in range(groups)]
    ids, sent = early(ids, tiles)
    asked, firsts = [None], []
    for k in range(1, groups):
        asked.append(lax.ppermute(ids, "x", swaps[k]))
    for k in range(1, groups):
        firsts.append(lax.ppermute(sent, "x", swaps[k]))
    received = [[None] * groups for _ in range(world_tiles)]
    for k in range(1, groups):
        payload = select(asked[k], tiles)
        for w in range(world_tiles):
            received[w][k] = lax.ppermute(payload[w], "x", swaps[k])

    mats, columns = prepare(
        stencil.reshape(world_tiles * 2, 2, cells),
        frac.reshape(world_tiles * 2, 2, cells),
        coef.reshape(world_tiles, 12, cells),
        pix,
    )

    carry = None
    for w in range(world_tiles):
        carry = world(w, ids, tiles, firsts, received[w][1:], mats, columns, carry)
    velocity, mine, other = carry
    total_rows = groups * lax.axis_size("y") * lax.axis_size("z") * 2 * world_tiles * 3 * cells
    halves = sum_devices(mine, other, F32(1.0 / total_rows))
    return (velocity.reshape(1, 1, world_tiles, 3, cells, snaps), factor(*halves, snaps))


def solution(mesh):
    grid = Mesh(mesh.devices.reshape(4, 4, 2, 4), ("y", "z", "core", "x"))
    columns = ("y", "z", "core")
    in_specs = (
        P("x", columns, None, None, None, None),
        P("x", columns, None, None),
        P("x", columns, None, None, None, None),
        P("x", columns, None, None, None, None),
        P("x", columns, None, None, None, None),
    )
    out_specs = (P("x", columns, None, None, None, None), P())
    return jax.shard_map(program, mesh=grid, in_specs=in_specs, out_specs=out_specs, check_vma=False)
```

```python
import functools

import jax
import jax.numpy as jnp
from jax import lax
from jax.experimental import pallas as pl
from jax.experimental.pallas import tpu as pltpu
from jax.sharding import Mesh, PartitionSpec as P


F32 = jnp.float32
BF16 = jnp.bfloat16
TILE_SIDE = 16
EARLY = 32
HALVES = (((0, 3), (1, 3), (2, 3), (3, 3), (0, 0)), ((0, 2), (1, 2), (2, 2), (0, 1), (1, 1)))
PLACE = {block: (half, at) for half, blocks in enumerate(HALVES) for at, block in enumerate(blocks)}
PLANE = ("y", "z")
ANY = pl.BlockSpec(memory_space=pl.ANY)
VM = pl.BlockSpec(memory_space=pltpu.VMEM)


def catmull(t):
    k0 = ((-0.5 * t + 1.0) * t - 0.5) * t
    k1 = (1.5 * t - 2.5) * t * t + 1.0
    k2 = ((-1.5 * t + 2.0) * t + 0.5) * t
    k3 = (0.5 * t - 0.5) * t * t
    return (k0, k1, k2, k3)


def prepare_kernel(sten_ref, frac_ref, coef_ref, mats_ref, columns_ref):
    pairs, cells = sten_ref.shape[0], sten_ref.shape[2]
    pix = mats_ref.shape[3]
    rows = []
    for p in range(pairs):
        for axis in range(2):
            rows.append(sten_ref[p, axis : axis + 1, :].astype(F32))
            rows.extend(catmull(frac_ref[p, axis : axis + 1, :]))
    for w in range(coef_ref.shape[0]):
        rows.append(coef_ref[w])
    used = sum(r.shape[0] for r in rows)
    rows.append(jnp.zeros((128 - used, cells), F32))
    table = jnp.concatenate(rows, axis=0).T
    columns_ref[...] = table
    lane = lax.broadcasted_iota(jnp.int32, (cells, pix), 1)
    spots = ((lane // TILE_SIDE).astype(F32), (lane % TILE_SIDE).astype(F32))
    for p in range(pairs):
        product = None
        for axis in range(2):
            at = 10 * p + 5 * axis
            offset = spots[axis] - table[:, at : at + 1]
            weight = jnp.zeros((cells, pix), F32)
            for shift in range(4):
                weight = jnp.where(offset == float(shift), table[:, at + 1 + shift : at + 2 + shift], weight)
            product = weight if product is None else product * weight
        mats_ref[p // 2, p % 2] = product.astype(BF16)


def prepare(sten, frac, coef, pix):
    pairs, _, cells = sten.shape
    return pl.pallas_call(
        prepare_kernel,
        out_shape=(
            jax.ShapeDtypeStruct((pairs // 2, 2, cells, pix), BF16),
            jax.ShapeDtypeStruct((cells, 128), F32),
        ),
        in_specs=[VM] * 3,
        out_specs=(VM, VM),
        compiler_params=pltpu.CompilerParams(vmem_limit_bytes=8 << 20),
        cost_estimate=pl.CostEstimate(flops=4_000_000, bytes_accessed=1_000_000, transcendentals=0),
        name="prepare",
    )(sten, frac, coef)


def early_kernel(ids_ref, cam_ref, ids_out, out, sem, ids_sem):
    copies = [pltpu.make_async_copy(cam_ref.at[t, :, pl.ds(0, EARLY)], out.at[t], sem.at[t]) for t in range(cam_ref.shape[0])]
    for copy in copies:
        copy.start()
    ids_copy = pltpu.make_async_copy(ids_ref, ids_out, ids_sem)
    ids_copy.start()
    for copy in copies:
        copy.wait()
    ids_copy.wait()


def early(ids, tiles):
    count, parts, _, snaps = tiles.shape
    return pl.pallas_call(
        early_kernel,
        out_shape=[jax.ShapeDtypeStruct(ids.shape, ids.dtype), jax.ShapeDtypeStruct((count, parts, EARLY, snaps), tiles.dtype)],
        in_specs=[ANY, ANY],
        out_specs=[VM, VM],
        scratch_shapes=[pltpu.SemaphoreType.DMA((count,)), pltpu.SemaphoreType.DMA],
        compiler_params=pltpu.CompilerParams(vmem_limit_bytes=4 << 20),
        cost_estimate=pl.CostEstimate(flops=0, bytes_accessed=500_000, transcendentals=0),
        name="early",
    )(ids, tiles)


def select_kernel(ids_ref, cam_ref, *rest):
    outs, sem = rest[:-1], rest[-1]
    me = lax.axis_index("x")
    count, _, pix, _ = cam_ref.shape
    copies = []
    for w, out in enumerate(outs):
        first, second = ids_ref[w, 0], ids_ref[w, 1]
        own = lax.shift_right_logical(first, 2) == me
        index = jnp.where(own, first, second) & (count - 1)
        copies.append(pltpu.make_async_copy(cam_ref.at[index, :, pl.ds(EARLY, pix - EARLY)], out, sem.at[w]))
        copies[-1].start()
    for copy in copies:
        copy.wait()


def select(ids, tiles):
    world_tiles = ids.shape[0]
    _, parts, pix, snaps = tiles.shape
    return pl.pallas_call(
        select_kernel,
        out_shape=[jax.ShapeDtypeStruct((parts, pix - EARLY, snaps), tiles.dtype)] * world_tiles,
        in_specs=[pl.BlockSpec(memory_space=pltpu.SMEM), ANY],
        out_specs=[VM] * world_tiles,
        scratch_shapes=[pltpu.SemaphoreType.DMA((world_tiles,))],
        compiler_params=pltpu.CompilerParams(vmem_limit_bytes=4 << 20),
        cost_estimate=pl.CostEstimate(flops=0, bytes_accessed=2_000_000, transcendentals=0),
    )(ids, tiles)


def world_kernel(w, ids_ref, cam_ref, e1_ref, e2_ref, e3_ref, r1_ref, r2_ref, r3_ref, mats_ref, coef_ref, *rest):
    if w:
        gin_ref, _, vel_ref, mine_ref, other_ref, tiles, interp, sem = rest
    else:
        vel_ref, gram_ref, tiles, interp, sem = rest
    cells, snaps = vel_ref.shape[2], vel_ref.shape[3]
    firsts, others = (None, e1_ref, e2_ref, e3_ref), (None, r1_ref, r2_ref, r3_ref)
    indices, dists = [], []
    for c in range(2):
        tile = ids_ref[w, c]
        index, dist = tile & 3, lax.shift_right_logical(tile, 2) ^ lax.axis_index("x")
        indices.append(index)
        dists.append(dist)

        @pl.when(dist == 0)
        def _():
            pltpu.make_async_copy(cam_ref.at[index], tiles.at[c], sem.at[c]).start()

    for c in range(2):
        for k in range(4):

            @pl.when(dists[c] == k)
            def _():
                if k == 0:
                    pltpu.make_async_copy(cam_ref.at[0], tiles.at[c], sem.at[c]).wait()
                else:
                    tiles[c, :, :EARLY] = firsts[k][indices[c]]
                    tiles[c, :, EARLY:] = others[k][...]

        for j in range(2):
            interp[2 * c + j] = jnp.dot(mats_ref[w, c], tiles[c, j], preferred_element_type=F32)

    rows = 32

    def cell_rows(step, _):
        q = pl.ds(pl.multiple_of(step * rows, rows), rows)
        parts = [interp[i, q, :] for i in range(4)]
        for k in range(3):
            at = 40 + 12 * w + 4 * k
            total = coef_ref[q, at : at + 1] * parts[0]
            for i in range(1, 4):
                total = total + coef_ref[q, at + i : at + i + 1] * parts[i]
            vel_ref[0, k, q, :] = total.astype(BF16)
        return 0

    lax.fori_loop(0, cells // rows, cell_rows, 0)
    flat = vel_ref[0].reshape(3 * cells, snaps)
    core = lax.axis_index("core")
    for i in range(snaps // 256):
        left = flat[:, 256 * i : 256 * (i + 1)]
        block = lax.dot_general(left, flat[:, 256 * i :], (((0,), (0,)), ((), ())), preferred_element_type=F32)
        parts = []
        for row in (2 * i, 2 * i + 1):
            for column in range(row, snaps // 128):
                half, at = PLACE[row, column]
                part = block[128 * row - 256 * i : 128 * (row + 1) - 256 * i, 128 * column - 256 * i : 128 * (column + 1) - 256 * i]
                if w == 0:
                    gram_ref[half, at] = part
                else:
                    parts.append((half, at, part + gin_ref[half, at]))
        if w == 0:
            continue
        for side in range(2):

            @pl.when(core == side)
            def _():
                for half, at, part in parts:
                    (mine_ref if half == side else other_ref)[at] = part


def world(w, ids, cam, firsts, recv, mats, coef, carry):
    snaps, cells = cam.shape[-1], mats.shape[2]
    world_tiles = 2
    outs = 2 if w else 1
    grams = (len(HALVES[0]), 128, 128) if w else (2, len(HALVES[0]), 128, 128)
    in_specs = [pl.BlockSpec(memory_space=pltpu.SMEM), ANY] + [VM] * 8
    args = [ids, cam, *firsts, *recv, mats, coef]
    aliases = {}
    if w:
        in_specs += [VM, ANY]
        args += [carry[1], carry[0]]
        aliases = {len(args) - 1: 0}
    return pl.pallas_call(
        functools.partial(world_kernel, w),
        grid=(1,),
        in_specs=in_specs,
        out_specs=(
            pl.BlockSpec((1, 3, cells, snaps), lambda _: (w, 0, 0, 0)),
            *[pl.BlockSpec(grams, lambda _: (0,) * len(grams))] * outs,
        ),
        out_shape=(
            jax.ShapeDtypeStruct((world_tiles, 3, cells, snaps), BF16),
            *[jax.ShapeDtypeStruct(grams, F32)] * outs,
        ),
        scratch_shapes=[
            pltpu.VMEM((2, 2, cam.shape[2], snaps), BF16),
            pltpu.VMEM((4, cells, snaps), F32),
            pltpu.SemaphoreType.DMA((2,)),
        ],
        input_output_aliases=aliases,
        compiler_params=pltpu.CompilerParams(vmem_limit_bytes=16 << 20),
        cost_estimate=pl.CostEstimate(flops=700_000_000, bytes_accessed=4_000_000, transcendentals=0),
    )(*args)


def spread(x, k):
    return jnp.broadcast_to(x[k % 8 : k % 8 + 1, :], x.shape)


def inverse_factor(blocks, size=16):
    width, per = blocks[0].shape[1], size // 8
    lane = lax.broadcasted_iota(jnp.int32, (8, width), 1)
    sub = lax.broadcasted_iota(jnp.int32, (8, width), 0)
    is_row = [sub == k for k in range(8)]
    slabs, out = list(blocks), []
    for s in range(len(blocks) // per):
        k0 = size * s
        own = slabs[s * per : (s + 1) * per]
        columns = [[jnp.broadcast_to(a[:, k0 + j : k0 + j + 1], (8, width)) for a in own] for j in range(size)]
        inside = (lane >= k0) & (lane < k0 + size)
        rows = [jnp.where(inside, jnp.where(lane - k0 - 8 * v == sub, 1.0, 0.0), a) for v, a in enumerate(own)]
        scaled = [None] * per
        for k in range(size):
            at, here = k // 8, is_row[k % 8]

            def fill(parts, value):
                return [jnp.where(here, value, x) if v == at else x for v, x in enumerate(parts)]

            pivot, row = fill(columns[k], -1.0), spread(rows[at], k)
            root = lax.rsqrt(spread(columns[k][at], k))
            pivot = [x * root for x in pivot]
            final = row * root
            scaled[at] = final if scaled[at] is None else jnp.where(here, final, scaled[at])
            for j in range(k + 1, size):
                ct = spread(columns[j][at], k) * root
                columns[j] = [x - pivot[v] * ct for v, x in enumerate(fill(columns[j], 0.0))]
            rows = [x - pivot[v] * final for v, x in enumerate(fill(rows, 0.0))]
        out.extend(jnp.where(lane < k0 + size, x, 0.0) for x in scaled)
        solved = [spread(rows[k // 8], k) for k in range(size)]
        for b in range((s + 1) * per, len(blocks)):
            x = slabs[b]
            totals = [jnp.where(inside, 0.0, x), 0.0]
            for k in range(size):
                totals[k % 2] = totals[k % 2] - jnp.broadcast_to(x[:, k0 + k : k0 + k + 1], (8, width)) * solved[k]
            slabs[b] = totals[0] + totals[1]
    return out


def exact_dot(a, b, dims):
    return lax.dot_general(a, b, ((dims[:1], dims[1:]), ((), ())), precision=lax.Precision.HIGHEST, preferred_element_type=F32)


def factor_kernel(own_ref, other_ref, o_ref, s_ref):
    n, size = o_ref.shape[0], 128
    parts = n // size
    core = lax.axis_index("core")
    for side in range(2):

        @pl.when(core == side)
        def _():
            for half, ref in ((side, own_ref), (1 - side, other_ref)):
                for at, (row, column) in enumerate(HALVES[half]):
                    s_ref[row * size : (row + 1) * size, column * size : (column + 1) * size] = ref[at]

    o_ref[...] = jnp.zeros_like(o_ref)

    def panel(p, _):
        off = pl.multiple_of(p * size, size)
        blocks = [s_ref[pl.ds(off + 8 * i, 8), pl.ds(off, size)] for i in range(size // 8)]
        linv = jnp.concatenate(inverse_factor(blocks), axis=0)
        for q in range(parts):

            @pl.when(p == q)
            def _():
                lo, wide = q * size, n - q * size
                r = exact_dot(linv, s_ref[lo : lo + size, lo:], (1, 0))
                row = lax.broadcasted_iota(jnp.int32, (size, wide), 0)
                col = lax.broadcasted_iota(jnp.int32, (size, wide), 1)
                r = jnp.where(col >= row, r, 0.0)
                o_ref[lo : lo + size, lo:] = r
                if q < parts - 1:
                    for m in range(q + 1, parts):
                        at = m * size
                        t = r[:, at - lo :]
                        s_ref[at : at + size, at:] = s_ref[at : at + size, at:] - exact_dot(t[:, :size], t, (0, 0))

        return 0

    lax.fori_loop(0, parts, panel, 0)


def factor(own, other, n):
    return pl.pallas_call(
        factor_kernel,
        out_shape=jax.ShapeDtypeStruct((n, n), F32),
        in_specs=[VM, VM],
        out_specs=VM,
        scratch_shapes=[pltpu.VMEM((n, n), F32)],
        compiler_params=pltpu.CompilerParams(vmem_limit_bytes=16 << 20),
        name="factor",
    )(own, other)


def sum_devices(mine, other, scale):
    planes = lax.axis_size("y") * lax.axis_size("z")
    groups = lax.axis_size("x")
    shape = mine.shape
    swap = [(0, 1), (1, 0)]
    mine = mine + lax.ppermute(other, "core", swap)
    pieces = lax.all_to_all(mine.reshape(planes, -1, 128), PLANE, 0, 0)
    piece = jnp.sum(pieces, axis=0)
    for k in (1, 2):
        piece = piece + lax.ppermute(piece, "x", [(i, i ^ k) for i in range(groups)])
    whole = lax.all_to_all(jnp.broadcast_to(piece * scale, pieces.shape), PLANE, 0, 0).reshape(shape)
    return whole, lax.ppermute(whole, "core", swap)


def program(cam_disp, footprint, stencil, frac, coef):
    cam_count, pix, snaps = cam_disp.shape[2], cam_disp.shape[4], cam_disp.shape[5]
    world_tiles = footprint.shape[2]
    cells = coef.shape[-1]
    groups = lax.axis_size("x")
    tiles = cam_disp.reshape(cam_count, 2, pix, snaps)
    tiles = pltpu.with_memory_space_constraint(tiles, pltpu.HBM)
    ids = pltpu.with_memory_space_constraint(footprint.reshape(world_tiles, 2), pltpu.HBM)

    swaps = [[(i, i ^ k) for i in range(groups)] for k in range(groups)]
    ids, sent = early(ids, tiles)
    asked, firsts = [None], []
    for k in range(1, groups):
        asked.append(lax.ppermute(ids, "x", swaps[k]))
    for k in range(1, groups):
        firsts.append(lax.ppermute(sent, "x", swaps[k]))
    received = [[None] * groups for _ in range(world_tiles)]
    for k in range(1, groups):
        payload = select(asked[k], tiles)
        for w in range(world_tiles):
            received[w][k] = lax.ppermute(payload[w], "x", swaps[k])

    mats, columns = prepare(
        stencil.reshape(world_tiles * 2, 2, cells),
        frac.reshape(world_tiles * 2, 2, cells),
        coef.reshape(world_tiles, 12, cells),
        pix,
    )

    carry = None
    for w in range(world_tiles):
        carry = world(w, ids, tiles, firsts, received[w][1:], mats, columns, carry)
    velocity, mine, other = carry
    total_rows = groups * lax.axis_size("y") * lax.axis_size("z") * 2 * world_tiles * 3 * cells
    halves = sum_devices(mine, other, F32(1.0 / total_rows))
    return (velocity.reshape(1, 1, world_tiles, 3, cells, snaps), factor(*halves, snaps))


def solution(mesh):
    grid = Mesh(mesh.devices.reshape(4, 4, 2, 4), ("y", "z", "core", "x"))
    columns = ("y", "z", "core")
    in_specs = (
        P("x", columns, None, None, None, None),
        P("x", columns, None, None),
        P("x", columns, None, None, None, None),
        P("x", columns, None, None, None, None),
        P("x", columns, None, None, None, None),
    )
    out_specs = (P("x", columns, None, None, None, None), P())
    return jax.shard_map(program, mesh=grid, in_specs=in_specs, out_specs=out_specs, check_vma=False)
```

```python
import functools

import jax
import jax.numpy as jnp
from jax import lax
from jax.experimental import pallas as pl
from jax.experimental.pallas import tpu as pltpu
from jax.sharding import Mesh, PartitionSpec as P


F32 = jnp.float32
BF16 = jnp.bfloat16
TILE_SIDE = 16
EARLY = 32
HALVES = (((0, 3), (1, 3), (2, 3), (3, 3), (0, 0)), ((0, 2), (1, 2), (2, 2), (0, 1), (1, 1)))
PLACE = {block: (half, at) for half, blocks in enumerate(HALVES) for at, block in enumerate(blocks)}
PLANE = ("y", "z")
ANY = pl.BlockSpec(memory_space=pl.ANY)
VM = pl.BlockSpec(memory_space=pltpu.VMEM)


def catmull(t):
    k0 = ((-0.5 * t + 1.0) * t - 0.5) * t
    k1 = (1.5 * t - 2.5) * t * t + 1.0
    k2 = ((-1.5 * t + 2.0) * t + 0.5) * t
    k3 = (0.5 * t - 0.5) * t * t
    return (k0, k1, k2, k3)


def prepare_kernel(sten_ref, frac_ref, coef_ref, mats_ref, columns_ref):
    pairs, cells = sten_ref.shape[0], sten_ref.shape[2]
    pix = mats_ref.shape[3]
    rows = []
    for p in range(pairs):
        for axis in range(2):
            rows.append(sten_ref[p, axis : axis + 1, :].astype(F32))
            rows.extend(catmull(frac_ref[p, axis : axis + 1, :]))
    for w in range(coef_ref.shape[0]):
        rows.append(coef_ref[w])
    used = sum(r.shape[0] for r in rows)
    rows.append(jnp.zeros((128 - used, cells), F32))
    table = jnp.concatenate(rows, axis=0).T
    columns_ref[...] = table
    lane = lax.broadcasted_iota(jnp.int32, (cells, pix), 1)
    spots = ((lane // TILE_SIDE).astype(F32), (lane % TILE_SIDE).astype(F32))
    for p in range(pairs):
        product = None
        for axis in range(2):
            at = 10 * p + 5 * axis
            offset = spots[axis] - table[:, at : at + 1]
            weight = jnp.zeros((cells, pix), F32)
            for shift in range(4):
                weight = jnp.where(offset == float(shift), table[:, at + 1 + shift : at + 2 + shift], weight)
            product = weight if product is None else product * weight
        mats_ref[p // 2, p % 2] = product.astype(BF16)


def prepare(sten, frac, coef, pix):
    pairs, _, cells = sten.shape
    return pl.pallas_call(
        prepare_kernel,
        out_shape=(
            jax.ShapeDtypeStruct((pairs // 2, 2, cells, pix), BF16),
            jax.ShapeDtypeStruct((cells, 128), F32),
        ),
        in_specs=[VM] * 3,
        out_specs=(VM, VM),
        compiler_params=pltpu.CompilerParams(vmem_limit_bytes=8 << 20),
        cost_estimate=pl.CostEstimate(flops=4_000_000, bytes_accessed=1_000_000, transcendentals=0),
        name="prepare",
    )(sten, frac, coef)


def early_kernel(ids_ref, cam_ref, ids_out, out, sem, ids_sem):
    copies = [pltpu.make_async_copy(cam_ref.at[t, :, pl.ds(0, EARLY)], out.at[t], sem.at[t]) for t in range(cam_ref.shape[0])]
    for copy in copies:
        copy.start()
    ids_copy = pltpu.make_async_copy(ids_ref, ids_out, ids_sem)
    ids_copy.start()
    for copy in copies:
        copy.wait()
    ids_copy.wait()


def early(ids, tiles):
    count, parts, _, snaps = tiles.shape
    return pl.pallas_call(
        early_kernel,
        out_shape=[jax.ShapeDtypeStruct(ids.shape, ids.dtype), jax.ShapeDtypeStruct((count, parts, EARLY, snaps), tiles.dtype)],
        in_specs=[ANY, ANY],
        out_specs=[VM, VM],
        scratch_shapes=[pltpu.SemaphoreType.DMA((count,)), pltpu.SemaphoreType.DMA],
        compiler_params=pltpu.CompilerParams(vmem_limit_bytes=4 << 20),
        cost_estimate=pl.CostEstimate(flops=0, bytes_accessed=500_000, transcendentals=0),
        name="early",
    )(ids, tiles)


def select_kernel(ids_ref, cam_ref, *rest):
    outs, sem = rest[:-1], rest[-1]
    me = lax.axis_index("x")
    count, _, pix, _ = cam_ref.shape
    copies = []
    for w, out in enumerate(outs):
        first, second = ids_ref[w, 0], ids_ref[w, 1]
        own = lax.shift_right_logical(first, 2) == me
        index = jnp.where(own, first, second) & (count - 1)
        copies.append(pltpu.make_async_copy(cam_ref.at[index, :, pl.ds(EARLY, pix - EARLY)], out, sem.at[w]))
        copies[-1].start()
    for copy in copies:
        copy.wait()


def select(ids, tiles):
    world_tiles = ids.shape[0]
    _, parts, pix, snaps = tiles.shape
    return pl.pallas_call(
        select_kernel,
        out_shape=[jax.ShapeDtypeStruct((parts, pix - EARLY, snaps), tiles.dtype)] * world_tiles,
        in_specs=[pl.BlockSpec(memory_space=pltpu.SMEM), ANY],
        out_specs=[VM] * world_tiles,
        scratch_shapes=[pltpu.SemaphoreType.DMA((world_tiles,))],
        compiler_params=pltpu.CompilerParams(vmem_limit_bytes=4 << 20),
        cost_estimate=pl.CostEstimate(flops=0, bytes_accessed=2_000_000, transcendentals=0),
    )(ids, tiles)


def world_kernel(w, ids_ref, cam_ref, e1_ref, e2_ref, e3_ref, r1_ref, r2_ref, r3_ref, mats_ref, coef_ref, *rest):
    if w:
        gin_ref, _, vel_out, mine_ref, other_ref, tiles, interp, vel_ref, sem, out_sem = rest
    else:
        vel_out, gram_ref, tiles, interp, vel_ref, sem, out_sem = rest
    _, cells, snaps = vel_ref.shape
    firsts, others = (None, e1_ref, e2_ref, e3_ref), (None, r1_ref, r2_ref, r3_ref)
    indices, dists = [], []
    for c in range(2):
        tile = ids_ref[w, c]
        index, dist = tile & 3, lax.shift_right_logical(tile, 2) ^ lax.axis_index("x")
        indices.append(index)
        dists.append(dist)

        @pl.when(dist == 0)
        def _():
            pltpu.make_async_copy(cam_ref.at[index], tiles.at[c], sem.at[c]).start()

    for c in range(2):
        for k in range(4):

            @pl.when(dists[c] == k)
            def _():
                if k == 0:
                    pltpu.make_async_copy(cam_ref.at[0], tiles.at[c], sem.at[c]).wait()
                else:
                    tiles[c, :, :EARLY] = firsts[k][indices[c]]
                    tiles[c, :, EARLY:] = others[k][...]

        for j in range(2):
            interp[2 * c + j] = jnp.dot(mats_ref[w, c], tiles[c, j], preferred_element_type=F32)

    rows = 32

    def cell_rows(step, _):
        q = pl.ds(pl.multiple_of(step * rows, rows), rows)
        parts = [interp[i, q, :] for i in range(4)]
        for k in range(3):
            at = 40 + 12 * w + 4 * k
            total = coef_ref[q, at : at + 1] * parts[0]
            for i in range(1, 4):
                total = total + coef_ref[q, at + i : at + i + 1] * parts[i]
            vel_ref[k, q, :] = total.astype(BF16)
        return 0

    lax.fori_loop(0, cells // rows, cell_rows, 0)
    leave = pltpu.make_async_copy(vel_ref, vel_out.at[w], out_sem)
    leave.start()
    flat = vel_ref[...].reshape(3 * cells, snaps)
    core = lax.axis_index("core")
    for i in range(snaps // 256):
        left = flat[:, 256 * i : 256 * (i + 1)]
        block = lax.dot_general(left, flat[:, 256 * i :], (((0,), (0,)), ((), ())), preferred_element_type=F32)
        parts = []
        for row in (2 * i, 2 * i + 1):
            for column in range(row, snaps // 128):
                half, at = PLACE[row, column]
                part = block[128 * row - 256 * i : 128 * (row + 1) - 256 * i, 128 * column - 256 * i : 128 * (column + 1) - 256 * i]
                if w == 0:
                    gram_ref[half, at] = part
                else:
                    parts.append((half, at, part + gin_ref[half, at]))
        for side in range(2 if w else 0):

            @pl.when(core == side)
            def _():
                for half, at, part in parts:
                    (mine_ref if half == side else other_ref)[at] = part

    leave.wait()


def world(w, ids, cam, firsts, recv, mats, coef, carry):
    snaps, cells = cam.shape[-1], mats.shape[2]
    world_tiles = 2
    outs = 2 if w else 1
    grams = (len(HALVES[0]), 128, 128) if w else (2, len(HALVES[0]), 128, 128)
    in_specs = [pl.BlockSpec(memory_space=pltpu.SMEM), ANY] + [VM] * 8
    args = [ids, cam, *firsts, *recv, mats, coef]
    aliases = {}
    if w:
        in_specs += [VM, ANY]
        args += [carry[1], carry[0]]
        aliases = {len(args) - 1: 0}
    return pl.pallas_call(
        functools.partial(world_kernel, w),
        in_specs=in_specs,
        out_specs=(
            ANY,
            *[VM] * outs,
        ),
        out_shape=(
            jax.ShapeDtypeStruct((world_tiles, 3, cells, snaps), BF16),
            *[jax.ShapeDtypeStruct(grams, F32)] * outs,
        ),
        scratch_shapes=[
            pltpu.VMEM((2, 2, cam.shape[2], snaps), BF16),
            pltpu.VMEM((4, cells, snaps), F32),
            pltpu.VMEM((3, cells, snaps), BF16),
            pltpu.SemaphoreType.DMA((2,)),
            pltpu.SemaphoreType.DMA,
        ],
        input_output_aliases=aliases,
        compiler_params=pltpu.CompilerParams(vmem_limit_bytes=16 << 20),
        cost_estimate=pl.CostEstimate(flops=700_000_000, bytes_accessed=4_000_000, transcendentals=0),
    )(*args)


def spread(x, k):
    return jnp.broadcast_to(x[k % 8 : k % 8 + 1, :], x.shape)


def inverse_factor(blocks, size=16):
    width, per = blocks[0].shape[1], size // 8
    lane = lax.broadcasted_iota(jnp.int32, (8, width), 1)
    sub = lax.broadcasted_iota(jnp.int32, (8, width), 0)
    is_row = [sub == k for k in range(8)]
    slabs, out = list(blocks), []
    for s in range(len(blocks) // per):
        k0 = size * s
        own = slabs[s * per : (s + 1) * per]
        columns = [[jnp.broadcast_to(a[:, k0 + j : k0 + j + 1], (8, width)) for a in own] for j in range(size)]
        inside = (lane >= k0) & (lane < k0 + size)
        rows = [jnp.where(inside, jnp.where(lane - k0 - 8 * v == sub, 1.0, 0.0), a) for v, a in enumerate(own)]
        scaled = [None] * per
        for k in range(size):
            at, here = k // 8, is_row[k % 8]

            def fill(parts, value):
                return [jnp.where(here, value, x) if v == at else x for v, x in enumerate(parts)]

            pivot, row = fill(columns[k], -1.0), spread(rows[at], k)
            root = lax.rsqrt(spread(columns[k][at], k))
            pivot = [x * root for x in pivot]
            final = row * root
            scaled[at] = final if scaled[at] is None else jnp.where(here, final, scaled[at])
            for j in range(k + 1, size):
                ct = spread(columns[j][at], k) * root
                columns[j] = [x - pivot[v] * ct for v, x in enumerate(fill(columns[j], 0.0))]
            rows = [x - pivot[v] * final for v, x in enumerate(fill(rows, 0.0))]
        out.extend(jnp.where(lane < k0 + size, x, 0.0) for x in scaled)
        solved = [spread(rows[k // 8], k) for k in range(size)]
        for b in range((s + 1) * per, len(blocks)):
            x = slabs[b]
            totals = [jnp.where(inside, 0.0, x), 0.0]
            for k in range(size):
                totals[k % 2] = totals[k % 2] - jnp.broadcast_to(x[:, k0 + k : k0 + k + 1], (8, width)) * solved[k]
            slabs[b] = totals[0] + totals[1]
    return out


def exact_dot(a, b, dims):
    return lax.dot_general(a, b, ((dims[:1], dims[1:]), ((), ())), precision=lax.Precision.HIGHEST, preferred_element_type=F32)


def factor_kernel(own_ref, other_ref, out_ref, s_ref, o_ref, sem):
    n, size = o_ref.shape[0], 128
    parts = n // size
    core = lax.axis_index("core")
    for side in range(2):

        @pl.when(core == side)
        def _():
            for half, ref in ((side, own_ref), (1 - side, other_ref)):
                for at, (row, column) in enumerate(HALVES[half]):
                    s_ref[row * size : (row + 1) * size, column * size : (column + 1) * size] = ref[at]

    o_ref[...] = jnp.zeros_like(o_ref)

    def leave(q):
        rows = pl.ds(q * size, size)
        return pltpu.make_async_copy(o_ref.at[rows], out_ref.at[rows], sem.at[q])

    def panel(p, _):
        off = pl.multiple_of(p * size, size)
        blocks = [s_ref[pl.ds(off + 8 * i, 8), pl.ds(off, size)] for i in range(size // 8)]
        linv = jnp.concatenate(inverse_factor(blocks), axis=0)
        for q in range(parts):

            @pl.when(p == q)
            def _():
                lo, wide = q * size, n - q * size
                r = exact_dot(linv, s_ref[lo : lo + size, lo:], (1, 0))
                row = lax.broadcasted_iota(jnp.int32, (size, wide), 0)
                col = lax.broadcasted_iota(jnp.int32, (size, wide), 1)
                r = jnp.where(col >= row, r, 0.0)
                o_ref[lo : lo + size, lo:] = r
                leave(q).start()
                if q < parts - 1:
                    for m in range(q + 1, parts):
                        at = m * size
                        t = r[:, at - lo :]
                        s_ref[at : at + size, at:] = s_ref[at : at + size, at:] - exact_dot(t[:, :size], t, (0, 0))

        return 0

    lax.fori_loop(0, parts, panel, 0)
    for q in range(parts):
        leave(q).wait()


def factor(own, other, n):
    return pl.pallas_call(
        factor_kernel,
        out_shape=jax.ShapeDtypeStruct((n, n), F32),
        in_specs=[VM, VM],
        out_specs=ANY,
        scratch_shapes=[pltpu.VMEM((n, n), F32), pltpu.VMEM((n, n), F32), pltpu.SemaphoreType.DMA((n // 128,))],
        compiler_params=pltpu.CompilerParams(vmem_limit_bytes=16 << 20),
        name="factor",
    )(own, other)


def sum_devices(mine, other, scale):
    planes = lax.axis_size("y") * lax.axis_size("z")
    groups = lax.axis_size("x")
    shape = mine.shape
    swap = [(0, 1), (1, 0)]
    mine = mine + lax.ppermute(other, "core", swap)
    pieces = lax.all_to_all(mine.reshape(planes, -1, 128), PLANE, 0, 0)
    piece = jnp.sum(pieces, axis=0)
    for k in (1, 2):
        piece = piece + lax.ppermute(piece, "x", [(i, i ^ k) for i in range(groups)])
    whole = lax.all_to_all(jnp.broadcast_to(piece * scale, pieces.shape), PLANE, 0, 0).reshape(shape)
    return whole, lax.ppermute(whole, "core", swap)


def program(cam_disp, footprint, stencil, frac, coef):
    cam_count, pix, snaps = cam_disp.shape[2], cam_disp.shape[4], cam_disp.shape[5]
    world_tiles = footprint.shape[2]
    cells = coef.shape[-1]
    groups = lax.axis_size("x")
    tiles = cam_disp.reshape(cam_count, 2, pix, snaps)
    tiles = pltpu.with_memory_space_constraint(tiles, pltpu.HBM)
    ids = pltpu.with_memory_space_constraint(footprint.reshape(world_tiles, 2), pltpu.HBM)

    swaps = [[(i, i ^ k) for i in range(groups)] for k in range(groups)]
    ids, sent = early(ids, tiles)
    asked, firsts = [None], []
    for k in range(1, groups):
        asked.append(lax.ppermute(ids, "x", swaps[k]))
    for k in range(1, groups):
        firsts.append(lax.ppermute(sent, "x", swaps[k]))
    received = [[None] * groups for _ in range(world_tiles)]
    for k in range(1, groups):
        payload = select(asked[k], tiles)
        for w in range(world_tiles):
            received[w][k] = lax.ppermute(payload[w], "x", swaps[k])

    mats, columns = prepare(
        stencil.reshape(world_tiles * 2, 2, cells),
        frac.reshape(world_tiles * 2, 2, cells),
        coef.reshape(world_tiles, 12, cells),
        pix,
    )

    carry = None
    for w in range(world_tiles):
        carry = world(w, ids, tiles, firsts, received[w][1:], mats, columns, carry)
    velocity, mine, other = carry
    total_rows = groups * lax.axis_size("y") * lax.axis_size("z") * 2 * world_tiles * 3 * cells
    halves = sum_devices(mine, other, F32(1.0 / total_rows))
    return (velocity.reshape(1, 1, world_tiles, 3, cells, snaps), factor(*halves, snaps))


def solution(mesh):
    grid = Mesh(mesh.devices.reshape(4, 4, 2, 4), ("y", "z", "core", "x"))
    columns = ("y", "z", "core")
    in_specs = (
        P("x", columns, None, None, None, None),
        P("x", columns, None, None),
        P("x", columns, None, None, None, None),
        P("x", columns, None, None, None, None),
        P("x", columns, None, None, None, None),
    )
    out_specs = (P("x", columns, None, None, None, None), P())
    return jax.shard_map(program, mesh=grid, in_specs=in_specs, out_specs=out_specs, check_vma=False)
```

```python
import functools

import jax
import jax.numpy as jnp
from jax import lax
from jax.experimental import pallas as pl
from jax.experimental.pallas import tpu as pltpu
from jax.sharding import Mesh, PartitionSpec as P


F32 = jnp.float32
BF16 = jnp.bfloat16
TILE_SIDE = 16
EARLY = 32
HALVES = (((0, 3), (1, 3), (2, 3), (3, 3), (0, 0)), ((0, 2), (1, 2), (2, 2), (0, 1), (1, 1)))
PLACE = {block: (half, at) for half, blocks in enumerate(HALVES) for at, block in enumerate(blocks)}
PLANE = ("y", "z")
ANY = pl.BlockSpec(memory_space=pl.ANY)
VM = pl.BlockSpec(memory_space=pltpu.VMEM)


def catmull(t):
    k0 = ((-0.5 * t + 1.0) * t - 0.5) * t
    k1 = (1.5 * t - 2.5) * t * t + 1.0
    k2 = ((-1.5 * t + 2.0) * t + 0.5) * t
    k3 = (0.5 * t - 0.5) * t * t
    return (k0, k1, k2, k3)


def prepare_kernel(sten_ref, frac_ref, coef_ref, mats_ref, columns_ref):
    pairs, cells = sten_ref.shape[0], sten_ref.shape[2]
    pix = mats_ref.shape[3]
    rows = []
    for p in range(pairs):
        for axis in range(2):
            rows.append(sten_ref[p, axis : axis + 1, :].astype(F32))
            rows.extend(catmull(frac_ref[p, axis : axis + 1, :]))
    for w in range(coef_ref.shape[0]):
        rows.append(coef_ref[w])
    used = sum(r.shape[0] for r in rows)
    rows.append(jnp.zeros((128 - used, cells), F32))
    table = jnp.concatenate(rows, axis=0).T
    columns_ref[...] = table
    lane = lax.broadcasted_iota(jnp.int32, (cells, pix), 1)
    spots = ((lane // TILE_SIDE).astype(F32), (lane % TILE_SIDE).astype(F32))
    for p in range(pairs):
        product = None
        for axis in range(2):
            at = 10 * p + 5 * axis
            offset = spots[axis] - table[:, at : at + 1]
            weight = jnp.zeros((cells, pix), F32)
            for shift in range(4):
                weight = jnp.where(offset == float(shift), table[:, at + 1 + shift : at + 2 + shift], weight)
            product = weight if product is None else product * weight
        mats_ref[p // 2, p % 2] = product.astype(BF16)


def prepare(sten, frac, coef, pix):
    pairs, _, cells = sten.shape
    return pl.pallas_call(
        prepare_kernel,
        out_shape=(
            jax.ShapeDtypeStruct((pairs // 2, 2, cells, pix), BF16),
            jax.ShapeDtypeStruct((cells, 128), F32),
        ),
        in_specs=[VM] * 3,
        out_specs=(VM, VM),
        compiler_params=pltpu.CompilerParams(vmem_limit_bytes=8 << 20),
        cost_estimate=pl.CostEstimate(flops=4_000_000, bytes_accessed=1_000_000, transcendentals=0),
        name="prepare",
    )(sten, frac, coef)


def early_kernel(ids_ref, cam_ref, ids_out, out, sem, ids_sem):
    copies = [pltpu.make_async_copy(cam_ref.at[t, :, pl.ds(0, EARLY)], out.at[t], sem.at[t]) for t in range(cam_ref.shape[0])]
    for copy in copies:
        copy.start()
    ids_copy = pltpu.make_async_copy(ids_ref, ids_out, ids_sem)
    ids_copy.start()
    for copy in copies:
        copy.wait()
    ids_copy.wait()


def early(ids, tiles):
    count, parts, _, snaps = tiles.shape
    return pl.pallas_call(
        early_kernel,
        out_shape=[jax.ShapeDtypeStruct(ids.shape, ids.dtype), jax.ShapeDtypeStruct((count, parts, EARLY, snaps), tiles.dtype)],
        in_specs=[ANY, ANY],
        out_specs=[VM, VM],
        scratch_shapes=[pltpu.SemaphoreType.DMA((count,)), pltpu.SemaphoreType.DMA],
        compiler_params=pltpu.CompilerParams(vmem_limit_bytes=4 << 20),
        cost_estimate=pl.CostEstimate(flops=0, bytes_accessed=500_000, transcendentals=0),
        name="early",
    )(ids, tiles)


def select_kernel(ids_ref, cam_ref, *rest):
    outs, sem = rest[:-1], rest[-1]
    me = lax.axis_index("x")
    count, _, pix, _ = cam_ref.shape
    copies = []
    for w, out in enumerate(outs):
        first, second = ids_ref[w, 0], ids_ref[w, 1]
        own = lax.shift_right_logical(first, 2) == me
        index = jnp.where(own, first, second) & (count - 1)
        copies.append(pltpu.make_async_copy(cam_ref.at[index, :, pl.ds(EARLY, pix - EARLY)], out, sem.at[w]))
        copies[-1].start()
    for copy in copies:
        copy.wait()


def select(ids, tiles):
    world_tiles = ids.shape[0]
    _, parts, pix, snaps = tiles.shape
    return pl.pallas_call(
        select_kernel,
        out_shape=[jax.ShapeDtypeStruct((parts, pix - EARLY, snaps), tiles.dtype)] * world_tiles,
        in_specs=[pl.BlockSpec(memory_space=pltpu.SMEM), ANY],
        out_specs=[VM] * world_tiles,
        scratch_shapes=[pltpu.SemaphoreType.DMA((world_tiles,))],
        compiler_params=pltpu.CompilerParams(vmem_limit_bytes=4 << 20),
        cost_estimate=pl.CostEstimate(flops=0, bytes_accessed=2_000_000, transcendentals=0),
    )(ids, tiles)


def world_kernel(w, ids_ref, e0_ref, e1_ref, e2_ref, e3_ref, r0_ref, r1_ref, r2_ref, r3_ref, mats_ref, coef_ref, *rest):
    if w:
        gin_ref, _, vel_out, mine_ref, other_ref, tiles, interp, vel_ref, out_sem = rest
    else:
        vel_out, gram_ref, tiles, interp, vel_ref, out_sem = rest
    _, cells, snaps = vel_ref.shape
    firsts, others = (e0_ref, e1_ref, e2_ref, e3_ref), (r0_ref, r1_ref, r2_ref, r3_ref)
    for c in range(2):
        tile = ids_ref[w, c]
        index, dist = tile & 3, lax.shift_right_logical(tile, 2) ^ lax.axis_index("x")
        for k in range(4):

            @pl.when(dist == k)
            def _():
                tiles[c, :, :EARLY] = firsts[k][index]
                tiles[c, :, EARLY:] = others[k][...]

        for j in range(2):
            interp[2 * c + j] = jnp.dot(mats_ref[w, c], tiles[c, j], preferred_element_type=F32)

    rows = 32

    def cell_rows(step, _):
        q = pl.ds(pl.multiple_of(step * rows, rows), rows)
        parts = [interp[i, q, :] for i in range(4)]
        for k in range(3):
            at = 40 + 12 * w + 4 * k
            total = coef_ref[q, at : at + 1] * parts[0]
            for i in range(1, 4):
                total = total + coef_ref[q, at + i : at + i + 1] * parts[i]
            vel_ref[k, q, :] = total.astype(BF16)
        pltpu.make_async_copy(vel_ref.at[:, q, :], vel_out.at[w, :, q, :], out_sem).start()
        return 0

    lax.fori_loop(0, cells // rows, cell_rows, 0)
    flat = vel_ref[...].reshape(3 * cells, snaps)
    core = lax.axis_index("core")
    for i in range(snaps // 256):
        left = flat[:, 256 * i : 256 * (i + 1)]
        block = lax.dot_general(left, flat[:, 256 * i :], (((0,), (0,)), ((), ())), preferred_element_type=F32)
        parts = []
        for row in (2 * i, 2 * i + 1):
            for column in range(row, snaps // 128):
                half, at = PLACE[row, column]
                part = block[128 * row - 256 * i : 128 * (row + 1) - 256 * i, 128 * column - 256 * i : 128 * (column + 1) - 256 * i]
                if w == 0:
                    gram_ref[half, at] = part
                else:
                    parts.append((half, at, part + gin_ref[half, at]))
        for side in range(2 if w else 0):

            @pl.when(core == side)
            def _():
                for half, at, part in parts:
                    (mine_ref if half == side else other_ref)[at] = part

    pltpu.make_async_copy(vel_ref, vel_out.at[w], out_sem).wait()


def world(w, ids, firsts, recv, mats, coef, carry):
    snaps, cells, pix = firsts[0].shape[-1], mats.shape[2], mats.shape[3]
    world_tiles = 2
    outs = 2 if w else 1
    grams = (len(HALVES[0]), 128, 128) if w else (2, len(HALVES[0]), 128, 128)
    in_specs = [pl.BlockSpec(memory_space=pltpu.SMEM)] + [VM] * 10
    args = [ids, *firsts, *recv, mats, coef]
    aliases = {}
    if w:
        in_specs += [VM, ANY]
        args += [carry[1], carry[0]]
        aliases = {len(args) - 1: 0}
    return pl.pallas_call(
        functools.partial(world_kernel, w),
        in_specs=in_specs,
        out_specs=(
            ANY,
            *[VM] * outs,
        ),
        out_shape=(
            jax.ShapeDtypeStruct((world_tiles, 3, cells, snaps), BF16),
            *[jax.ShapeDtypeStruct(grams, F32)] * outs,
        ),
        scratch_shapes=[
            pltpu.VMEM((2, 2, pix, snaps), BF16),
            pltpu.VMEM((4, cells, snaps), F32),
            pltpu.VMEM((3, cells, snaps), BF16),
            pltpu.SemaphoreType.DMA,
        ],
        input_output_aliases=aliases,
        compiler_params=pltpu.CompilerParams(vmem_limit_bytes=16 << 20),
        cost_estimate=pl.CostEstimate(flops=700_000_000, bytes_accessed=4_000_000, transcendentals=0),
    )(*args)


def spread(x, k):
    return jnp.broadcast_to(x[k % 8 : k % 8 + 1, :], x.shape)


def inverse_factor(blocks, size=16):
    width, per = blocks[0].shape[1], size // 8
    lane = lax.broadcasted_iota(jnp.int32, (8, width), 1)
    sub = lax.broadcasted_iota(jnp.int32, (8, width), 0)
    is_row = [sub == k for k in range(8)]
    slabs, out = list(blocks), []
    for s in range(len(blocks) // per):
        k0 = size * s
        own = slabs[s * per : (s + 1) * per]
        columns = [[jnp.broadcast_to(a[:, k0 + j : k0 + j + 1], (8, width)) for a in own] for j in range(size)]
        inside = (lane >= k0) & (lane < k0 + size)
        rows = [jnp.where(inside, jnp.where(lane - k0 - 8 * v == sub, 1.0, 0.0), a) for v, a in enumerate(own)]
        scaled = [None] * per
        for k in range(size):
            at, here = k // 8, is_row[k % 8]

            def fill(parts, value):
                return [jnp.where(here, value, x) if v == at else x for v, x in enumerate(parts)]

            pivot, row = fill(columns[k], -1.0), spread(rows[at], k)
            root = lax.rsqrt(spread(columns[k][at], k))
            pivot = [x * root for x in pivot]
            final = row * root
            scaled[at] = final if scaled[at] is None else jnp.where(here, final, scaled[at])
            for j in range(k + 1, size):
                ct = spread(columns[j][at], k) * root
                columns[j] = [x - pivot[v] * ct for v, x in enumerate(fill(columns[j], 0.0))]
            rows = [x - pivot[v] * final for v, x in enumerate(fill(rows, 0.0))]
        out.extend(jnp.where(lane < k0 + size, x, 0.0) for x in scaled)
        solved = [spread(rows[k // 8], k) for k in range(size)]
        for b in range((s + 1) * per, len(blocks)):
            x = slabs[b]
            totals = [jnp.where(inside, 0.0, x), 0.0]
            for k in range(size):
                totals[k % 2] = totals[k % 2] - jnp.broadcast_to(x[:, k0 + k : k0 + k + 1], (8, width)) * solved[k]
            slabs[b] = totals[0] + totals[1]
    return out


def exact_dot(a, b, dims):
    return lax.dot_general(a, b, ((dims[:1], dims[1:]), ((), ())), precision=lax.Precision.HIGHEST, preferred_element_type=F32)


def factor_kernel(own_ref, other_ref, out_ref, s_ref, o_ref, sem):
    n, size = o_ref.shape[0], 128
    parts = n // size
    core = lax.axis_index("core")
    for side in range(2):

        @pl.when(core == side)
        def _():
            for half, ref in ((side, own_ref), (1 - side, other_ref)):
                for at, (row, column) in enumerate(HALVES[half]):
                    s_ref[row * size : (row + 1) * size, column * size : (column + 1) * size] = ref[at]

    o_ref[...] = jnp.zeros_like(o_ref)

    def leave(q, zeros):
        where = (pl.ds(q * size, size), pl.ds(0, q * size) if zeros else pl.ds(q * size, n - q * size))
        return pltpu.make_async_copy(o_ref.at[where], out_ref.at[where], sem.at[int(zeros), q])

    for q in range(1, parts):
        leave(q, True).start()

    def panel(p, _):
        off = pl.multiple_of(p * size, size)
        blocks = [s_ref[pl.ds(off + 8 * i, 8), pl.ds(off, size)] for i in range(size // 8)]
        linv = jnp.concatenate(inverse_factor(blocks), axis=0)
        for q in range(parts):

            @pl.when(p == q)
            def _():
                lo, wide = q * size, n - q * size
                r = exact_dot(linv, s_ref[lo : lo + size, lo:], (1, 0))
                row = lax.broadcasted_iota(jnp.int32, (size, wide), 0)
                col = lax.broadcasted_iota(jnp.int32, (size, wide), 1)
                r = jnp.where(col >= row, r, 0.0)
                o_ref[lo : lo + size, lo:] = r
                leave(q, False).start()
                if q < parts - 1:
                    for m in range(q + 1, parts):
                        at = m * size
                        t = r[:, at - lo :]
                        s_ref[at : at + size, at:] = s_ref[at : at + size, at:] - exact_dot(t[:, :size], t, (0, 0))

        return 0

    lax.fori_loop(0, parts, panel, 0)
    for q in range(parts):
        leave(q, False).wait()
        if q:
            leave(q, True).wait()


def factor(own, other, n):
    return pl.pallas_call(
        factor_kernel,
        out_shape=jax.ShapeDtypeStruct((n, n), F32),
        in_specs=[VM, VM],
        out_specs=ANY,
        scratch_shapes=[pltpu.VMEM((n, n), F32), pltpu.VMEM((n, n), F32), pltpu.SemaphoreType.DMA((2, n // 128))],
        compiler_params=pltpu.CompilerParams(vmem_limit_bytes=16 << 20),
        name="factor",
    )(own, other)


def sum_devices(mine, other, scale):
    planes = lax.axis_size("y") * lax.axis_size("z")
    groups = lax.axis_size("x")
    shape = mine.shape
    swap = [(0, 1), (1, 0)]
    mine = mine + lax.ppermute(other, "core", swap)
    pieces = lax.all_to_all(mine.reshape(planes, -1, 128), PLANE, 0, 0)
    piece = jnp.sum(pieces, axis=0)
    for k in (1, 2):
        piece = piece + lax.ppermute(piece, "x", [(i, i ^ k) for i in range(groups)])
    whole = lax.all_to_all(jnp.broadcast_to(piece * scale, pieces.shape), PLANE, 0, 0).reshape(shape)
    return whole, lax.ppermute(whole, "core", swap)


def program(cam_disp, footprint, stencil, frac, coef):
    cam_count, pix, snaps = cam_disp.shape[2], cam_disp.shape[4], cam_disp.shape[5]
    world_tiles = footprint.shape[2]
    cells = coef.shape[-1]
    groups = lax.axis_size("x")
    tiles = cam_disp.reshape(cam_count, 2, pix, snaps)
    tiles = pltpu.with_memory_space_constraint(tiles, pltpu.HBM)
    ids = pltpu.with_memory_space_constraint(footprint.reshape(world_tiles, 2), pltpu.HBM)

    swaps = [[(i, i ^ k) for i in range(groups)] for k in range(groups)]
    ids, sent = early(ids, tiles)
    asked, firsts = [ids], [sent]
    for k in range(1, groups):
        asked.append(lax.ppermute(ids, "x", swaps[k]))
    for k in range(1, groups):
        firsts.append(lax.ppermute(sent, "x", swaps[k]))
    received = [[None] * groups for _ in range(world_tiles)]
    for k in range(1, groups):
        payload = select(asked[k], tiles)
        for w in range(world_tiles):
            received[w][k] = lax.ppermute(payload[w], "x", swaps[k])

    for w, tile in enumerate(select(ids, tiles)):
        received[w][0] = tile

    mats, columns = prepare(
        stencil.reshape(world_tiles * 2, 2, cells),
        frac.reshape(world_tiles * 2, 2, cells),
        coef.reshape(world_tiles, 12, cells),
        pix,
    )

    carry = None
    for w in range(world_tiles):
        carry = world(w, ids, firsts, received[w], mats, columns, carry)
    velocity, mine, other = carry
    total_rows = groups * lax.axis_size("y") * lax.axis_size("z") * 2 * world_tiles * 3 * cells
    halves = sum_devices(mine, other, F32(1.0 / total_rows))
    return (velocity.reshape(1, 1, world_tiles, 3, cells, snaps), factor(*halves, snaps))


def solution(mesh):
    grid = Mesh(mesh.devices.reshape(4, 4, 2, 4), ("y", "z", "core", "x"))
    columns = ("y", "z", "core")
    in_specs = (
        P("x", columns, None, None, None, None),
        P("x", columns, None, None),
        P("x", columns, None, None, None, None),
        P("x", columns, None, None, None, None),
        P("x", columns, None, None, None, None),
    )
    out_specs = (P("x", columns, None, None, None, None), P())
    return jax.shard_map(program, mesh=grid, in_specs=in_specs, out_specs=out_specs, check_vma=False)
```

```python
import functools

import jax
import jax.numpy as jnp
from jax import lax
from jax.experimental import pallas as pl
from jax.experimental.pallas import tpu as pltpu
from jax.sharding import Mesh, PartitionSpec as P


F32 = jnp.float32
BF16 = jnp.bfloat16
TILE_SIDE = 16
EARLY = 16
HALVES = (((0, 3), (1, 3), (2, 3), (3, 3), (0, 0)), ((0, 2), (1, 2), (2, 2), (0, 1), (1, 1)))
PLACE = {block: (half, at) for half, blocks in enumerate(HALVES) for at, block in enumerate(blocks)}
PLANE = ("y", "z")
ANY = pl.BlockSpec(memory_space=pl.ANY)
VM = pl.BlockSpec(memory_space=pltpu.VMEM)


def catmull(t):
    k0 = ((-0.5 * t + 1.0) * t - 0.5) * t
    k1 = (1.5 * t - 2.5) * t * t + 1.0
    k2 = ((-1.5 * t + 2.0) * t + 0.5) * t
    k3 = (0.5 * t - 0.5) * t * t
    return (k0, k1, k2, k3)


def prepare_kernel(sten_ref, frac_ref, coef_ref, mats_ref, columns_ref):
    pairs, cells = sten_ref.shape[0], sten_ref.shape[2]
    pix = mats_ref.shape[3]
    rows = []
    for p in range(pairs):
        for axis in range(2):
            rows.append(sten_ref[p, axis : axis + 1, :].astype(F32))
            rows.extend(catmull(frac_ref[p, axis : axis + 1, :]))
    for w in range(coef_ref.shape[0]):
        rows.append(coef_ref[w])
    used = sum(r.shape[0] for r in rows)
    rows.append(jnp.zeros((128 - used, cells), F32))
    table = jnp.concatenate(rows, axis=0).T
    columns_ref[...] = table
    lane = lax.broadcasted_iota(jnp.int32, (cells, pix), 1)
    spots = ((lane // TILE_SIDE).astype(F32), (lane % TILE_SIDE).astype(F32))
    for p in range(pairs):
        product = None
        for axis in range(2):
            at = 10 * p + 5 * axis
            offset = spots[axis] - table[:, at : at + 1]
            weight = jnp.zeros((cells, pix), F32)
            for shift in range(4):
                weight = jnp.where(offset == float(shift), table[:, at + 1 + shift : at + 2 + shift], weight)
            product = weight if product is None else product * weight
        mats_ref[p // 2, p % 2] = product.astype(BF16)


def prepare(sten, frac, coef, pix):
    pairs, _, cells = sten.shape
    return pl.pallas_call(
        prepare_kernel,
        out_shape=(
            jax.ShapeDtypeStruct((pairs // 2, 2, cells, pix), BF16),
            jax.ShapeDtypeStruct((cells, 128), F32),
        ),
        in_specs=[VM] * 3,
        out_specs=(VM, VM),
        compiler_params=pltpu.CompilerParams(vmem_limit_bytes=8 << 20),
        cost_estimate=pl.CostEstimate(flops=4_000_000, bytes_accessed=1_000_000, transcendentals=0),
        name="prepare",
    )(sten, frac, coef)


def early_kernel(ids_ref, cam_ref, ids_out, out, sem, ids_sem):
    copies = [pltpu.make_async_copy(cam_ref.at[t, :, pl.ds(0, EARLY)], out.at[t], sem.at[t]) for t in range(cam_ref.shape[0])]
    for copy in copies:
        copy.start()
    ids_copy = pltpu.make_async_copy(ids_ref, ids_out, ids_sem)
    ids_copy.start()
    for copy in copies:
        copy.wait()
    ids_copy.wait()


def early(ids, tiles):
    count, parts, _, snaps = tiles.shape
    return pl.pallas_call(
        early_kernel,
        out_shape=[jax.ShapeDtypeStruct(ids.shape, ids.dtype), jax.ShapeDtypeStruct((count, parts, EARLY, snaps), tiles.dtype)],
        in_specs=[ANY, ANY],
        out_specs=[VM, VM],
        scratch_shapes=[pltpu.SemaphoreType.DMA((count,)), pltpu.SemaphoreType.DMA],
        compiler_params=pltpu.CompilerParams(vmem_limit_bytes=4 << 20),
        cost_estimate=pl.CostEstimate(flops=0, bytes_accessed=500_000, transcendentals=0),
        name="early",
    )(ids, tiles)


def select_kernel(ids_ref, cam_ref, *rest):
    outs, sem = rest[:-1], rest[-1]
    me = lax.axis_index("x")
    count, _, pix, _ = cam_ref.shape
    copies = []
    for w, out in enumerate(outs):
        first, second = ids_ref[w, 0], ids_ref[w, 1]
        own = lax.shift_right_logical(first, 2) == me
        index = jnp.where(own, first, second) & (count - 1)
        copies.append(pltpu.make_async_copy(cam_ref.at[index, :, pl.ds(EARLY, pix - EARLY)], out, sem.at[w]))
        copies[-1].start()
    for copy in copies:
        copy.wait()


def select(ids, tiles):
    world_tiles = ids.shape[0]
    _, parts, pix, snaps = tiles.shape
    return pl.pallas_call(
        select_kernel,
        out_shape=[jax.ShapeDtypeStruct((parts, pix - EARLY, snaps), tiles.dtype)] * world_tiles,
        in_specs=[pl.BlockSpec(memory_space=pltpu.SMEM), ANY],
        out_specs=[VM] * world_tiles,
        scratch_shapes=[pltpu.SemaphoreType.DMA((world_tiles,))],
        compiler_params=pltpu.CompilerParams(vmem_limit_bytes=4 << 20),
        cost_estimate=pl.CostEstimate(flops=0, bytes_accessed=2_000_000, transcendentals=0),
    )(ids, tiles)


def world_kernel(w, ids_ref, e0_ref, e1_ref, e2_ref, e3_ref, r0_ref, r1_ref, r2_ref, r3_ref, mats_ref, coef_ref, *rest):
    if w:
        gin_ref, _, vel_out, mine_ref, other_ref, tiles, interp, vel_ref, out_sem = rest
    else:
        vel_out, gram_ref, tiles, interp, vel_ref, out_sem = rest
    _, cells, snaps = vel_ref.shape
    firsts, others = (e0_ref, e1_ref, e2_ref, e3_ref), (r0_ref, r1_ref, r2_ref, r3_ref)
    for c in range(2):
        tile = ids_ref[w, c]
        index, dist = tile & 3, lax.shift_right_logical(tile, 2) ^ lax.axis_index("x")
        for k in range(4):

            @pl.when(dist == k)
            def _():
                tiles[c, :, :EARLY] = firsts[k][index]
                tiles[c, :, EARLY:] = others[k][...]

        for j in range(2):
            interp[2 * c + j] = jnp.dot(mats_ref[w, c], tiles[c, j], preferred_element_type=F32)

    rows = 32

    def cell_rows(step, _):
        q = pl.ds(pl.multiple_of(step * rows, rows), rows)
        parts = [interp[i, q, :] for i in range(4)]
        for k in range(3):
            at = 40 + 12 * w + 4 * k
            total = coef_ref[q, at : at + 1] * parts[0]
            for i in range(1, 4):
                total = total + coef_ref[q, at + i : at + i + 1] * parts[i]
            vel_ref[k, q, :] = total.astype(BF16)
        pltpu.make_async_copy(vel_ref.at[:, q, :], vel_out.at[w, :, q, :], out_sem).start()
        return 0

    lax.fori_loop(0, cells // rows, cell_rows, 0)
    flat = vel_ref[...].reshape(3 * cells, snaps)
    core = lax.axis_index("core")
    for i in range(snaps // 256):
        left = flat[:, 256 * i : 256 * (i + 1)]
        block = lax.dot_general(left, flat[:, 256 * i :], (((0,), (0,)), ((), ())), preferred_element_type=F32)
        parts = []
        for row in (2 * i, 2 * i + 1):
            for column in range(row, snaps // 128):
                half, at = PLACE[row, column]
                part = block[128 * row - 256 * i : 128 * (row + 1) - 256 * i, 128 * column - 256 * i : 128 * (column + 1) - 256 * i]
                if w == 0:
                    gram_ref[half, at] = part
                else:
                    parts.append((half, at, part + gin_ref[half, at]))
        for side in range(2 if w else 0):

            @pl.when(core == side)
            def _():
                for half, at, part in parts:
                    (mine_ref if half == side else other_ref)[at] = part

    pltpu.make_async_copy(vel_ref, vel_out.at[w], out_sem).wait()


def world(w, ids, firsts, recv, mats, coef, carry):
    snaps, cells, pix = firsts[0].shape[-1], mats.shape[2], mats.shape[3]
    world_tiles = 2
    outs = 2 if w else 1
    grams = (len(HALVES[0]), 128, 128) if w else (2, len(HALVES[0]), 128, 128)
    in_specs = [pl.BlockSpec(memory_space=pltpu.SMEM)] + [VM] * 10
    args = [ids, *firsts, *recv, mats, coef]
    aliases = {}
    if w:
        in_specs += [VM, ANY]
        args += [carry[1], carry[0]]
        aliases = {len(args) - 1: 0}
    return pl.pallas_call(
        functools.partial(world_kernel, w),
        in_specs=in_specs,
        out_specs=(
            ANY,
            *[VM] * outs,
        ),
        out_shape=(
            jax.ShapeDtypeStruct((world_tiles, 3, cells, snaps), BF16),
            *[jax.ShapeDtypeStruct(grams, F32)] * outs,
        ),
        scratch_shapes=[
            pltpu.VMEM((2, 2, pix, snaps), BF16),
            pltpu.VMEM((4, cells, snaps), F32),
            pltpu.VMEM((3, cells, snaps), BF16),
            pltpu.SemaphoreType.DMA,
        ],
        input_output_aliases=aliases,
        compiler_params=pltpu.CompilerParams(vmem_limit_bytes=16 << 20),
        cost_estimate=pl.CostEstimate(flops=700_000_000, bytes_accessed=4_000_000, transcendentals=0),
    )(*args)


def spread(x, k):
    return jnp.broadcast_to(x[k % 8 : k % 8 + 1, :], x.shape)


def inverse_factor(blocks, size=16):
    width, per = blocks[0].shape[1], size // 8
    lane = lax.broadcasted_iota(jnp.int32, (8, width), 1)
    sub = lax.broadcasted_iota(jnp.int32, (8, width), 0)
    is_row = [sub == k for k in range(8)]
    slabs, out = list(blocks), []
    for s in range(len(blocks) // per):
        k0 = size * s
        own = slabs[s * per : (s + 1) * per]
        columns = [[jnp.broadcast_to(a[:, k0 + j : k0 + j + 1], (8, width)) for a in own] for j in range(size)]
        inside = (lane >= k0) & (lane < k0 + size)
        rows = [jnp.where(inside, jnp.where(lane - k0 - 8 * v == sub, 1.0, 0.0), a) for v, a in enumerate(own)]
        scaled = [None] * per
        diagonal = spread(columns[0][0], 0)
        for k in range(size):
            at, here = k // 8, is_row[k % 8]

            def fill(parts, value):
                return [jnp.where(here, value, x) if v == at else x for v, x in enumerate(parts)]

            pivot, row = fill(columns[k], -1.0), spread(rows[at], k)
            root = lax.rsqrt(diagonal)
            if k + 1 < size:
                below, v = spread(columns[k][(k + 1) // 8], k + 1) * root, (k + 1) // 8
                diagonal = spread(columns[k + 1][v], k + 1) - below * below
            pivot = [x * root for x in pivot]
            final = row * root
            scaled[at] = final if scaled[at] is None else jnp.where(here, final, scaled[at])
            for j in range(k + 1, size):
                ct = spread(columns[j][at], k) * root
                columns[j] = [x - pivot[v] * ct for v, x in enumerate(fill(columns[j], 0.0))]
            rows = [x - pivot[v] * final for v, x in enumerate(fill(rows, 0.0))]
        out.extend(jnp.where(lane < k0 + size, x, 0.0) for x in scaled)
        solved = [spread(rows[k // 8], k) for k in range(size)]
        for b in range((s + 1) * per, len(blocks)):
            x = slabs[b]
            totals = [jnp.where(inside, 0.0, x), 0.0]
            for k in range(size):
                totals[k % 2] = totals[k % 2] - jnp.broadcast_to(x[:, k0 + k : k0 + k + 1], (8, width)) * solved[k]
            slabs[b] = totals[0] + totals[1]
    return out


def exact_dot(a, b, dims):
    return lax.dot_general(a, b, ((dims[:1], dims[1:]), ((), ())), precision=lax.Precision.HIGHEST, preferred_element_type=F32)


def factor_kernel(own_ref, other_ref, out_ref, s_ref, o_ref, sem):
    n, size = o_ref.shape[0], 128
    parts = n // size
    core = lax.axis_index("core")
    for side in range(2):

        @pl.when(core == side)
        def _():
            for half, ref in ((side, own_ref), (1 - side, other_ref)):
                for at, (row, column) in enumerate(HALVES[half]):
                    s_ref[row * size : (row + 1) * size, column * size : (column + 1) * size] = ref[at]

    o_ref[...] = jnp.zeros_like(o_ref)

    def leave(q, zeros):
        where = (pl.ds(q * size, size), pl.ds(0, q * size) if zeros else pl.ds(q * size, n - q * size))
        return pltpu.make_async_copy(o_ref.at[where], out_ref.at[where], sem.at[int(zeros), q])

    for q in range(1, parts):
        leave(q, True).start()

    def panel(p, _):
        off = pl.multiple_of(p * size, size)
        blocks = [s_ref[pl.ds(off + 8 * i, 8), pl.ds(off, size)] for i in range(size // 8)]
        linv = jnp.concatenate(inverse_factor(blocks), axis=0)
        for q in range(parts):

            @pl.when(p == q)
            def _():
                lo, wide = q * size, n - q * size
                r = exact_dot(linv, s_ref[lo : lo + size, lo:], (1, 0))
                row = lax.broadcasted_iota(jnp.int32, (size, wide), 0)
                col = lax.broadcasted_iota(jnp.int32, (size, wide), 1)
                r = jnp.where(col >= row, r, 0.0)
                o_ref[lo : lo + size, lo:] = r
                leave(q, False).start()
                if q < parts - 1:
                    for m in range(q + 1, parts):
                        at = m * size
                        t = r[:, at - lo :]
                        s_ref[at : at + size, at:] = s_ref[at : at + size, at:] - exact_dot(t[:, :size], t, (0, 0))

        return 0

    lax.fori_loop(0, parts, panel, 0)
    for q in range(parts):
        leave(q, False).wait()
        if q:
            leave(q, True).wait()


def factor(own, other, n):
    return pl.pallas_call(
        factor_kernel,
        out_shape=jax.ShapeDtypeStruct((n, n), F32),
        in_specs=[VM, VM],
        out_specs=ANY,
        scratch_shapes=[pltpu.VMEM((n, n), F32), pltpu.VMEM((n, n), F32), pltpu.SemaphoreType.DMA((2, n // 128))],
        compiler_params=pltpu.CompilerParams(vmem_limit_bytes=16 << 20),
        name="factor",
    )(own, other)


def sum_devices(mine, other, scale):
    planes = lax.axis_size("y") * lax.axis_size("z")
    groups = lax.axis_size("x")
    shape = mine.shape
    swap = [(0, 1), (1, 0)]
    mine = mine + lax.ppermute(other, "core", swap)
    pieces = lax.all_to_all(mine.reshape(planes, -1, 128), PLANE, 0, 0)
    piece = jnp.sum(pieces, axis=0)
    for k in (1, 2):
        piece = piece + lax.ppermute(piece, "x", [(i, i ^ k) for i in range(groups)])
    whole = lax.all_to_all(jnp.broadcast_to(piece * scale, pieces.shape), PLANE, 0, 0).reshape(shape)
    return whole, lax.ppermute(whole, "core", swap)


def program(cam_disp, footprint, stencil, frac, coef):
    cam_count, pix, snaps = cam_disp.shape[2], cam_disp.shape[4], cam_disp.shape[5]
    world_tiles = footprint.shape[2]
    cells = coef.shape[-1]
    groups = lax.axis_size("x")
    tiles = cam_disp.reshape(cam_count, 2, pix, snaps)
    tiles = pltpu.with_memory_space_constraint(tiles, pltpu.HBM)
    ids = pltpu.with_memory_space_constraint(footprint.reshape(world_tiles, 2), pltpu.HBM)

    swaps = [[(i, i ^ k) for i in range(groups)] for k in range(groups)]
    ids, sent = early(ids, tiles)
    asked, firsts = [ids], [sent]
    for k in range(1, groups):
        asked.append(lax.ppermute(ids, "x", swaps[k]))
    for k in range(1, groups):
        firsts.append(lax.ppermute(sent, "x", swaps[k]))
    received = [[None] * groups for _ in range(world_tiles)]
    for k in range(1, groups):
        payload = select(asked[k], tiles)
        for w in range(world_tiles):
            received[w][k] = lax.ppermute(payload[w], "x", swaps[k])

    for w, tile in enumerate(select(ids, tiles)):
        received[w][0] = tile

    mats, columns = prepare(
        stencil.reshape(world_tiles * 2, 2, cells),
        frac.reshape(world_tiles * 2, 2, cells),
        coef.reshape(world_tiles, 12, cells),
        pix,
    )

    carry = None
    for w in range(world_tiles):
        carry = world(w, ids, firsts, received[w], mats, columns, carry)
    velocity, mine, other = carry
    total_rows = groups * lax.axis_size("y") * lax.axis_size("z") * 2 * world_tiles * 3 * cells
    halves = sum_devices(mine, other, F32(1.0 / total_rows))
    return (velocity.reshape(1, 1, world_tiles, 3, cells, snaps), factor(*halves, snaps))


def solution(mesh):
    grid = Mesh(mesh.devices.reshape(4, 4, 2, 4), ("y", "z", "core", "x"))
    columns = ("y", "z", "core")
    in_specs = (
        P("x", columns, None, None, None, None),
        P("x", columns, None, None),
        P("x", columns, None, None, None, None),
        P("x", columns, None, None, None, None),
        P("x", columns, None, None, None, None),
    )
    out_specs = (P("x", columns, None, None, None, None), P())
    return jax.shard_map(program, mesh=grid, in_specs=in_specs, out_specs=out_specs, check_vma=False)
```
